32 devices in a mesh: groups: 2 (over y), blk: 8 (over z, x), uly: 2 (over core).
Axes of the slice: x: 2, y: 2, z: 4, core: 2. Of those that a mesh axis runs over, the one named last changes fastest.
Arguments:
- query_proj: bfloat16 [4096, 4096], P(('groups', 'blk', 'uly')), parts along dimension 0, may hold values from -17 to 17
- key_proj: bfloat16 [4096, 512], P(('groups', 'blk', 'uly')), parts along dimension 0, may hold values from -17 to 17
- value_projection: bfloat16 [4096, 512], P(('groups', 'blk', 'uly')), parts along dimension 0, may hold values from -6 to 6
- query_gain: float32 [128], replicated, may hold values from 0.5 to 6
- key_gain: float32 [128], replicated, may hold values from 0.5 to 6
Outputs:
- attended: bfloat16 [4096, 4096], P(('groups', 'blk', 'uly')), parts along dimension 0
The draws below stay inside these ranges and needn't reach their ends.
There are 2 independent parts, one for each index of `groups`. The reference program is written for one: setup_inputs(seed, part) draws one part's arguments, and reference() takes and returns one part's arrays. A program takes and returns all parts, laid end to end along the dimension named above; an argument that names none is the same for every part. Nothing has to cross between parts.
All inputs are finite; a program needn't handle non-finite values.
Results may differ from the reference program's by a relative error of at most 0.0085.
The reference program's roundings to bfloat16 on the way count: a program that leaves them out, or rounds other values in their place, can miss the bound.
Values may be sent and summed in bfloat16 or wider, within the bound.
A program may use at most 64 MiB of HBM per device.

```python
import math
import jax
import jax.numpy as jnp
from jax import lax

STRETCH_TOKENS = 128
QUERY_HEADS = 32
KEY_VALUE_HEADS = 4
HEAD_SIZE = 128
WINDOW_TOKENS = 128
SEQUENCE_TOKENS = 2048
N_BLK = 8


def flagged_rows(key, row_count, head_count):
    sample = jnp.clip(jax.random.normal(key, (row_count, head_count, HEAD_SIZE), jnp.float32), -6.0, 6.0)
    return sample.reshape(row_count, head_count * HEAD_SIZE)


def gain_table(key, salt):
    own_key = jax.random.fold_in(key, salt)
    scales = jnp.exp(jax.random.uniform(own_key, (HEAD_SIZE,), jnp.float32, math.log(0.5), math.log(2.0)))
    return scales


def draw_query_proj(key, part):
    return flagged_rows(key, SEQUENCE_TOKENS, QUERY_HEADS).astype(jnp.bfloat16)


def draw_key_proj(key, part):
    return flagged_rows(key, SEQUENCE_TOKENS, KEY_VALUE_HEADS).astype(jnp.bfloat16)


def draw_query_gain(key, part):
    return gain_table(key, 101)


def draw_key_gain(key, part):
    return gain_table(key, 202)


def steps_of(stream_key, extent, cuts, least, largest):
    gain, own = 1.0, jax.random.fold_in(stream_key, 6)
    for dim, blocks in cuts:
        draws = jnp.exp(jax.random.uniform(jax.random.fold_in(own, dim), (blocks,), jnp.float32, least / len(cuts), largest / len(cuts)))
        gain = gain * jnp.repeat(draws, extent[dim] // blocks).reshape([-1 if axis == dim else 1 for axis in range(len(extent))])
    return gain


def normal_values(key, shape, width, bound, cuts=(), kind=jnp.bfloat16):
    array = jax.random.normal(key, shape, jnp.float32) * width
    if len(cuts) > 0:
        array = steps_of(key, shape, cuts, -0.22, 0.18) * array
    return jnp.clip(array, min=-bound, max=bound).astype(kind)


def setup_inputs(seed: int = 0, part: int = 0) -> dict:
    key_list = jax.random.split(jax.random.key(seed), 6)
    part_splits = jax.random.split(jax.random.fold_in(key_list[5], part), 6)
    return {
        "query_proj": draw_query_proj(jax.random.fold_in(jax.random.fold_in(key_list[5], part), 71), part),
        "key_proj": draw_key_proj(jax.random.fold_in(jax.random.fold_in(key_list[5], part), 71), part),
        "value_projection": normal_values(part_splits[2], (SEQUENCE_TOKENS, KEY_VALUE_HEADS * HEAD_SIZE), 1.0, 6.0, ((0, 16),)),
        "query_gain": draw_query_gain(jax.random.fold_in(key_list[5], 71), part),
        "key_gain": draw_key_gain(jax.random.fold_in(key_list[5], 71), part),
    }


NEG_FILL = -1e+30
ROPE_BASE = 1000000.0

def rotate_rows(source, scales, positions):
    head_width = scales.shape[0]
    row_count = source.shape[0]
    head_count = source.shape[1] // head_width
    values = source.astype(jnp.float32).reshape(row_count, head_count, head_width)
    mean_square = lax.optimization_barrier(jnp.mean(values * values, axis=-1, keepdims=True))
    normed = values * lax.rsqrt(mean_square + 1e-06) * scales.astype(jnp.float32)
    half_width = head_width // 2
    frequency = jnp.exp(jnp.arange(half_width, dtype=jnp.float32) * (-2.0 * math.log(ROPE_BASE) / head_width))
    angles = positions.astype(jnp.float32)[:, None] * frequency[None, :]
    cosine = jnp.cos(angles)[:, None, :]
    sine = jnp.sin(angles)[:, None, :]
    first_half = normed[..., :half_width]
    second_half = normed[..., half_width:]
    rotated = jnp.concatenate([first_half * cosine - second_half * sine, second_half * cosine + first_half * sine], axis=-1)
    return rotated.reshape(row_count, head_count * head_width).astype(jnp.bfloat16)

def reference(query_proj, key_proj, value_projection, query_gain, key_gain):
    seq_len = SEQUENCE_TOKENS
    stored = jnp.arange(seq_len, dtype=jnp.int32)
    stored_block = stored // STRETCH_TOKENS
    cycle_pos = stored_block // 2
    stretch_id = jnp.where(stored_block % 2 == 0, cycle_pos, 2 * N_BLK - 1 - cycle_pos)
    position = (stretch_id * STRETCH_TOKENS + stored % STRETCH_TOKENS).astype(jnp.int32)
    query_rot = rotate_rows(query_proj, query_gain, position)
    key_rot = rotate_rows(key_proj, key_gain, position)
    natural = jnp.arange(seq_len, dtype=jnp.int32)
    natural_stretch = natural // STRETCH_TOKENS
    stored_slot = jnp.where(natural_stretch < N_BLK, 2 * natural_stretch, 2 * (2 * N_BLK - 1 - natural_stretch) + 1)
    source = (stored_slot * STRETCH_TOKENS + natural % STRETCH_TOKENS).astype(jnp.int32)
    query_sequence = query_rot[source]
    key_sequence = key_rot[source]
    value_sequence = value_projection[source]
    key_padded = jnp.concatenate([jnp.zeros((WINDOW_TOKENS, KEY_VALUE_HEADS * HEAD_SIZE), jnp.bfloat16), key_sequence], axis=0)
    value_padded = jnp.concatenate([jnp.zeros((WINDOW_TOKENS, KEY_VALUE_HEADS * HEAD_SIZE), jnp.bfloat16), value_sequence], axis=0)
    group_count = QUERY_HEADS // KEY_VALUE_HEADS

    def one_stretch(stretch_index):
        starting_row = (stretch_index * STRETCH_TOKENS).astype(jnp.int32)
        query_tile = lax.dynamic_slice_in_dim(query_sequence, starting_row, STRETCH_TOKENS, 0).astype(jnp.float32).reshape(STRETCH_TOKENS, KEY_VALUE_HEADS, group_count, HEAD_SIZE)
        key_tile = lax.dynamic_slice_in_dim(key_padded, starting_row, WINDOW_TOKENS + STRETCH_TOKENS, 0).astype(jnp.float32).reshape(WINDOW_TOKENS + STRETCH_TOKENS, KEY_VALUE_HEADS, HEAD_SIZE)
        value_tile = lax.dynamic_slice_in_dim(value_padded, starting_row, WINDOW_TOKENS + STRETCH_TOKENS, 0).astype(jnp.float32).reshape(WINDOW_TOKENS + STRETCH_TOKENS, KEY_VALUE_HEADS, HEAD_SIZE)
        scores = jnp.einsum('rkgd,nkd->kgrn', query_tile, key_tile) * (1.0 / math.sqrt(HEAD_SIZE))
        query_pos = starting_row + jnp.arange(STRETCH_TOKENS, dtype=jnp.int32)
        key_pos = starting_row - WINDOW_TOKENS + jnp.arange(WINDOW_TOKENS + STRETCH_TOKENS, dtype=jnp.int32)
        distance = query_pos[:, None] - key_pos[None, :]
        allowed = (distance >= 0) & (distance < WINDOW_TOKENS) & (key_pos >= 0)[None, :]
        scores = jnp.where(allowed, scores, NEG_FILL)
        top_score = lax.optimization_barrier(jnp.max(scores, axis=-1, keepdims=True))
        weights = jnp.exp(scores - top_score)
        total_weight = lax.optimization_barrier(jnp.sum(weights, axis=-1))
        rounded = lax.optimization_barrier(weights.astype(jnp.bfloat16)).astype(jnp.float32)
        mixed_rows = jnp.einsum('kgrn,nkd->kgrd', rounded, value_tile) / total_weight[..., None]
        return jnp.transpose(mixed_rows, (2, 0, 1, 3)).reshape(STRETCH_TOKENS, QUERY_HEADS * HEAD_SIZE).astype(jnp.bfloat16)
    stretches = lax.map(one_stretch, jnp.arange(2 * N_BLK, dtype=jnp.int32))
    out_seq = stretches.reshape(seq_len, QUERY_HEADS * HEAD_SIZE)
    return out_seq[position]
```

```python
import functools
import math

import jax
import jax.numpy as jnp
from jax import lax
from jax.experimental import pallas as pl
from jax.experimental.pallas import tpu as pltpu
from jax.sharding import PartitionSpec as P

NEG_FILL = -1e30
ROPE_BASE = 1000000.0
EPS = 1e-06
MESH = pl.DeviceIdType.MESH


def angle_parts(stretch, rows, span, frequency):
    steps = rows // 8
    count = 8 + steps + 8 * pl.cdiv(span + 1, 8)
    index = lax.broadcasted_iota(jnp.int32, (count, frequency.shape[1]), 0)
    offset = jnp.where(
        index < 8,
        index,
        jnp.where(index < 8 + steps, (index - 8) * 8, (stretch - (index - 8 - steps)) * rows),
    )
    angle = offset.astype(jnp.float32) * frequency
    return jnp.cos(angle), jnp.sin(angle)


def rope_table(parts, d, rows):
    cosine, sine = parts
    steps = rows // 8
    fine_cos, fine_sin = cosine[:8], sine[:8]
    eights_cos, eights_sin = cosine[8 : 8 + steps], sine[8 : 8 + steps]
    at = 8 + steps + d
    first_cos, first_sin = cosine[at : at + 1], sine[at : at + 1]
    coarse_cos = eights_cos * first_cos - eights_sin * first_sin
    coarse_sin = eights_sin * first_cos + eights_cos * first_sin
    cosines, sines = [], []
    for j in range(steps):
        cos_j, sin_j = coarse_cos[j : j + 1], coarse_sin[j : j + 1]
        cosines.append(cos_j * fine_cos - sin_j * fine_sin)
        sines.append(sin_j * fine_cos + cos_j * fine_sin)
    return jnp.concatenate(cosines), jnp.concatenate(sines)


def rotate(x, table_a, table_b):
    x = x.astype(jnp.float32)
    r = lax.rsqrt(jnp.sum(x * x, axis=-1, keepdims=True) + x.shape[1] * EPS)
    swapped = pltpu.roll(x, x.shape[1] // 2, 1)
    return ((x * table_a + swapped * table_b) * r).astype(jnp.bfloat16)


def kernel(
    cycle, span, kv_heads, group,
    q_hbm, k_hbm, v_hbm, qg_hbm, kg_hbm, o_ref,
    q_buf, kv_own, kv_prev, q_rot, k_own, k_far, v_cat, tiles, weights, tab, gains,
    q_sem, own_sem, gain_sem, send_sem, recv_sem,
):
    rows, head = k_hbm.shape[0], qg_hbm.shape[1]
    width = group * head
    blk, uly = lax.axis_index("blk"), lax.axis_index("uly")
    last = 2 * cycle - 1
    stretch = jnp.where(uly == 0, blk, last - blk)

    def device_of(index):
        low = index < cycle
        return {"blk": jnp.where(low, index, last - index), "uly": jnp.where(low, 0, 1)}

    barrier = pltpu.get_barrier_semaphore()
    for d in range(1, span + 1):

        @pl.when(stretch >= d)
        def _(d=d):
            pl.semaphore_signal(
                barrier, inc=1, device_id=device_of(stretch - d), device_id_type=MESH
            )

    own_copies = [
        pltpu.make_async_copy(src, kv_own.at[i], own_sem.at[i])
        for i, src in enumerate((k_hbm, v_hbm))
    ]
    q_copies = [
        pltpu.make_async_copy(
            q_hbm.at[:, pl.ds(h * width, width)], q_buf.at[h], q_sem.at[h]
        )
        for h in range(kv_heads)
    ]
    gain_copies = [
        pltpu.make_async_copy(src, gains.at[i], gain_sem.at[i])
        for i, src in enumerate((qg_hbm, kg_hbm))
    ]

    def remote(d, h, i, src):
        return pltpu.make_async_remote_copy(
            src_ref=src.at[:, pl.ds(h * head, head)],
            dst_ref=kv_prev.at[d - 1, i, h],
            send_sem=send_sem.at[d - 1, i, h],
            recv_sem=recv_sem.at[d - 1, i, h],
            device_id=device_of(stretch + d),
            device_id_type=MESH,
        )

    from_hbm = (k_hbm, v_hbm)
    from_vmem = (kv_own.at[0], kv_own.at[1])

    def each_send(act, sources):
        for i in range(2):
            for h in range(kv_heads):
                for d in range(1, span + 1):

                    @pl.when(stretch + d <= last)
                    def _(d=d, h=h, i=i):
                        act(remote(d, h, i, sources[i]))

    for copy in own_copies + gain_copies + q_copies:
        copy.start()

    for d in range(1, span + 1):

        @pl.when(stretch < d)
        def _(d=d):
            for i in range(2):
                for h in range(kv_heads):
                    pltpu.make_async_copy(
                        from_hbm[i].at[:, pl.ds(h * head, head)],
                        kv_prev.at[d - 1, i, h],
                        recv_sem.at[d - 1, i, h],
                    ).start()

    half = head // 2
    lane = lax.broadcasted_iota(jnp.int32, (1, head), 1)
    frequency = jnp.exp(
        lax.rem(lane, half).astype(jnp.float32) * (-2.0 * math.log(ROPE_BASE) / head)
    )
    sign = jnp.where(lane < half, -1.0, 1.0)

    for d in range(1, span + 1):

        @pl.when(stretch + d <= last)
        def _():
            pl.semaphore_wait(barrier, 1)

    @pl.when(uly == 1)
    def _():
        each_send(lambda copy: copy.start(), from_hbm)

    for copy in own_copies:
        copy.wait()

    @pl.when(uly == 0)
    def _():
        each_send(lambda copy: copy.start(), from_vmem)

    parts = angle_parts(stretch, rows, span, frequency)
    for copy in gain_copies:
        copy.wait()
    q_gain, k_gain = gains[0] * math.sqrt(head), gains[1] * math.sqrt(head)
    q_swap, k_swap = sign * pltpu.roll(q_gain, half, 1), sign * pltpu.roll(k_gain, half, 1)
    for d in range(span + 1):
        cosine, sine = rope_table(parts, d, rows)
        tab[d + 1, 0], tab[d + 1, 1] = cosine * k_gain, sine * k_swap
        if d == 0:
            tab[0, 0], tab[0, 1] = cosine * q_gain, sine * q_swap

    row = lax.broadcasted_iota(jnp.int32, (rows, rows), 0)
    col = lax.broadcasted_iota(jnp.int32, (rows, rows), 1)
    own = col <= row
    contract = (((1,), (1,)), ((), ()))

    for h in range(kv_heads):
        k_own[h] = rotate(
            kv_own[0, :, h * head : (h + 1) * head], tab[1, 0], tab[1, 1]
        )
        v_cat[h, :rows, :head] = kv_own[1, :, h * head : (h + 1) * head]
        v_cat[h, :, head:] = jnp.ones_like(v_cat[h, :, head:])
    for h in range(kv_heads):
        q_copies[h].wait()
        keys = k_own[h]
        for g in range(group):
            at = slice(g * rows, (g + 1) * rows)
            q_rot[h, at] = rotate(
                q_buf[h, :, g * head : (g + 1) * head], tab[0, 0], tab[0, 1]
            )
            scores = lax.dot_general(
                q_rot[h, at], keys, contract, preferred_element_type=jnp.float32
            )
            tiles[h, 0, at] = jnp.where(own, scores, NEG_FILL)

    scale = math.log2(math.e) / math.sqrt(head)
    keep = col <= row + jnp.where(stretch >= span, 0, rows)
    own_mask = own.astype(jnp.float32).astype(jnp.bfloat16)
    far_mask = 1.0 - own_mask
    bias = [
        jnp.where(stretch >= d, 0.0, NEG_FILL).astype(jnp.float32)
        for d in range(1, span)
    ]

    def arrived(h, i):
        for d in range(1, span + 1):
            remote(d, h, i, from_hbm[i]).wait_recv()

    def score(h):
        for d in range(1, span + 1):
            k_far[h, (d - 1) * rows : d * rows] = rotate(
                kv_prev[d - 1, 0, h], tab[d + 1, 0], tab[d + 1, 1]
            )
        keys = k_far[h]
        for g in range(group):
            at = slice(g * rows, (g + 1) * rows)
            scores = lax.dot_general(
                q_rot[h, at], keys, contract, preferred_element_type=jnp.float32
            )
            tiles[h, 0, at] = jnp.where(
                keep, tiles[h, 0, at], scores[:, (span - 1) * rows :]
            )
            for d in range(1, span):
                tiles[h, d, at] = scores[:, (d - 1) * rows : d * rows] + bias[d - 1]

    def weigh(h):
        for g in range(group):
            at = slice(g * rows, (g + 1) * rows)
            parts = [tiles[h, d, at] for d in range(span)]
            top = jnp.max(functools.reduce(jnp.maximum, parts), axis=-1, keepdims=True)
            for d in range(span):
                weights[h, d, at] = jnp.exp2((parts[d] - top) * scale).astype(jnp.bfloat16)

    def mix(h):
        for d in range(1, span + 1):
            v_cat[h, d * rows : (d + 1) * rows, :head] = kv_prev[d - 1, 1, h]
        values = v_cat[h]
        for g in range(group):
            at = slice(g * rows, (g + 1) * rows)
            merged = weights[h, 0, at]
            spread = [merged * own_mask]
            spread += [weights[h, d, at] for d in range(1, span)]
            spread += [merged * far_mask]
            mixed = jnp.dot(
                jnp.concatenate(spread, axis=1), values, preferred_element_type=jnp.float32
            )
            o_ref[:, h * width + g * head : h * width + (g + 1) * head] = (
                mixed[:, :head] / mixed[:, head:]
            ).astype(o_ref.dtype)

    for h in range(kv_heads):
        arrived(h, 0)
        score(h)
        if h > 0:
            weigh(h - 1)
    for h in range(kv_heads):
        arrived(h, 1)
        if h == 0:
            weigh(kv_heads - 1)
        mix(h)

    @pl.when(uly == 1)
    def _():
        each_send(lambda copy: copy.wait_send(), from_hbm)

    @pl.when(uly == 0)
    def _():
        each_send(lambda copy: copy.wait_send(), from_vmem)


def in_hbm(array):
    return pltpu.with_memory_space_constraint(array, pltpu.HBM)


def local(query_proj, key_proj, value_projection, query_gain, key_gain):
    cycle = lax.axis_size("blk")
    span = max(1, cycle // 64)
    rows, head = query_proj.shape[0], query_gain.shape[0]
    kv_heads = key_proj.shape[1] // head
    group = query_proj.shape[1] // head // kv_heads
    bf16, f32 = jnp.bfloat16, jnp.float32
    vmem = pl.BlockSpec(memory_space=pltpu.VMEM)
    hbm = pl.BlockSpec(memory_space=pltpu.HBM)
    return pl.pallas_call(
        functools.partial(kernel, cycle, span, kv_heads, group),
        out_shape=jax.ShapeDtypeStruct(query_proj.shape, bf16),
        in_specs=[hbm] * 5,
        out_specs=vmem,
        scratch_shapes=[
            pltpu.VMEM((kv_heads, rows, group * head), bf16),
            pltpu.VMEM((2, rows, kv_heads * head), bf16),
            pltpu.VMEM((span, 2, kv_heads, rows, head), bf16),
            pltpu.VMEM((kv_heads, group * rows, head), bf16),
            pltpu.VMEM((kv_heads, rows, head), bf16),
            pltpu.VMEM((kv_heads, span * rows, head), bf16),
            pltpu.VMEM((kv_heads, (span + 1) * rows, 2 * head), bf16),
            pltpu.VMEM((kv_heads, span, group * rows, rows), f32),
            pltpu.VMEM((kv_heads, span, group * rows, rows), bf16),
            pltpu.VMEM((span + 2, 2, rows, head), f32),
            pltpu.VMEM((2, 1, head), f32),
            pltpu.SemaphoreType.DMA((kv_heads,)),
            pltpu.SemaphoreType.DMA((2,)),
            pltpu.SemaphoreType.DMA((2,)),
            pltpu.SemaphoreType.DMA((span, 2, kv_heads)),
            pltpu.SemaphoreType.DMA((span, 2, kv_heads)),
        ],
        compiler_params=pltpu.CompilerParams(
            collective_id=0, has_side_effects=True, vmem_limit_bytes=24 * 1024 * 1024
        ),
        name="window_attention",
    )(
        in_hbm(query_proj),
        in_hbm(key_proj),
        in_hbm(value_projection),
        in_hbm(query_gain.reshape(1, head)),
        in_hbm(key_gain.reshape(1, head)),
    )


def solution(mesh):
    rows = P(("groups", "blk", "uly"), None)
    return jax.shard_map(
        local,
        mesh=mesh,
        in_specs=(rows, rows, rows, P(), P()),
        out_specs=rows,
        check_vma=False,
    )
```

```python
import functools
import math

import jax
import jax.numpy as jnp
from jax import lax
from jax.experimental import pallas as pl
from jax.experimental.pallas import tpu as pltpu
from jax.sharding import PartitionSpec as P

NEG_FILL = -1e30
ROPE_BASE = 1000000.0
EPS = 1e-06
MESH = pl.DeviceIdType.MESH


def angle_parts(stretch, rows, span, frequency):
    steps = rows // 8
    count = 8 + steps + 8 * pl.cdiv(span + 1, 8)
    index = lax.broadcasted_iota(jnp.int32, (count, frequency.shape[1]), 0)
    offset = jnp.where(
        index < 8,
        index,
        jnp.where(index < 8 + steps, (index - 8) * 8, (stretch - (index - 8 - steps)) * rows),
    )
    angle = offset.astype(jnp.float32) * frequency
    return jnp.cos(angle), jnp.sin(angle)


def rope_table(parts, d, rows):
    cosine, sine = parts
    steps = rows // 8
    fine_cos, fine_sin = cosine[:8], sine[:8]
    eights_cos, eights_sin = cosine[8 : 8 + steps], sine[8 : 8 + steps]
    at = 8 + steps + d
    first_cos, first_sin = cosine[at : at + 1], sine[at : at + 1]
    coarse_cos = eights_cos * first_cos - eights_sin * first_sin
    coarse_sin = eights_sin * first_cos + eights_cos * first_sin
    cosines, sines = [], []
    for j in range(steps):
        cos_j, sin_j = coarse_cos[j : j + 1], coarse_sin[j : j + 1]
        cosines.append(cos_j * fine_cos - sin_j * fine_sin)
        sines.append(sin_j * fine_cos + cos_j * fine_sin)
    return jnp.concatenate(cosines), jnp.concatenate(sines)


def rotate(x, table_a, table_b, swap):
    swapped = jnp.dot(x, swap, preferred_element_type=jnp.float32)
    x = x.astype(jnp.float32)
    r = lax.rsqrt(jnp.sum(x * x, axis=-1, keepdims=True) + x.shape[1] * EPS)
    return ((x * table_a + swapped * table_b) * r).astype(jnp.bfloat16)


def kernel(
    cycle, span, kv_heads, group,
    q_hbm, k_hbm, v_hbm, qg_hbm, kg_hbm, o_ref,
    q_buf, kv_own, kv_prev, q_rot, k_own, k_far, v_cat, tiles, weights, tab, gains,
    relay_buf, q_sem, own_sem, gain_sem, send_sem, recv_sem, pass_sem, relay_sem,
):
    rows, head = k_hbm.shape[0], qg_hbm.shape[1]
    width = group * head
    blk, uly = lax.axis_index("blk"), lax.axis_index("uly")
    last = 2 * cycle - 1
    stretch = jnp.where(uly == 0, blk, last - blk)

    def device_of(index):
        low = index < cycle
        return {"blk": jnp.where(low, index, last - index), "uly": jnp.where(low, 0, 1)}

    def relayed_by(index):
        some = (index >= cycle) & (index + 2 <= last) & (lax.rem(index, 2) == 0)
        return jnp.where(some, jnp.where(index == cycle, kv_heads, kv_heads - 1), 0)

    to_relay = jnp.where(stretch >= 1, relayed_by(stretch - 1), 0)
    passed = relayed_by(stretch)
    from_relay = jnp.where(stretch >= 2, relayed_by(stretch - 2), 0)

    barrier = pltpu.get_barrier_semaphore()

    def greet(index):
        pl.semaphore_signal(
            barrier, inc=1, device_id=device_of(index), device_id_type=MESH
        )

    for d in range(1, span + 1):
        pl.when(stretch >= d)(functools.partial(greet, stretch - d))
    pl.when(from_relay > 0)(functools.partial(greet, stretch - 2))
    pl.when(passed > 0)(functools.partial(greet, stretch + 1))

    own_copies = [
        pltpu.make_async_copy(src, kv_own.at[i], own_sem.at[i])
        for i, src in enumerate((k_hbm, v_hbm))
    ]
    q_copies = [
        pltpu.make_async_copy(
            q_hbm.at[:, pl.ds(h * width, width)], q_buf.at[h], q_sem.at[h]
        )
        for h in range(kv_heads)
    ]
    gain_copies = [
        pltpu.make_async_copy(src, gains.at[i], gain_sem.at[i])
        for i, src in enumerate((qg_hbm, kg_hbm))
    ]

    def remote(d, h, i, src):
        return pltpu.make_async_remote_copy(
            src_ref=src.at[:, pl.ds(h * head, head)],
            dst_ref=kv_prev.at[d - 1, i, h],
            send_sem=send_sem.at[d - 1, i, h],
            recv_sem=recv_sem.at[d - 1, i, h],
            device_id=device_of(stretch + d),
            device_id_type=MESH,
        )

    from_hbm = (k_hbm, v_hbm)
    from_vmem = (kv_own.at[0], kv_own.at[1])

    def each_send(act, sources):
        for i in range(2):
            for h in range(kv_heads):
                for d in range(1, span + 1):
                    sent = stretch + d <= last
                    if d == 1 and i == 1:
                        sent = sent & (h < kv_heads - to_relay)

                    @pl.when(sent)
                    def _(d=d, h=h, i=i):
                        act(remote(d, h, i, sources[i]))

    def to_next_but_one(h):
        return pltpu.make_async_remote_copy(
            src_ref=relay_buf.at[h],
            dst_ref=kv_prev.at[0, 1, h],
            send_sem=pass_sem.at[h],
            recv_sem=recv_sem.at[0, 1, h],
            device_id=device_of(stretch + 2),
            device_id_type=MESH,
        )

    def by_relay(h):
        return pltpu.make_async_remote_copy(
            src_ref=v_hbm.at[:, pl.ds(h * head, head)],
            dst_ref=relay_buf.at[h],
            send_sem=send_sem.at[0, 1, h],
            recv_sem=relay_sem.at[h],
            device_id=device_of(stretch - 1),
            device_id_type=MESH,
        )

    def each_by_relay(act):
        for h in range(kv_heads):

            @pl.when(h >= kv_heads - to_relay)
            def _(h=h):
                act(by_relay(h))

    def pass_on(h):
        @pl.when(h >= kv_heads - passed)
        def _():
            by_relay(h).wait_recv()
            to_next_but_one(h).start()

    for copy in own_copies + gain_copies + q_copies:
        copy.start()

    for d in range(1, span + 1):

        @pl.when(stretch < d)
        def _(d=d):
            for i in range(2):
                for h in range(kv_heads):
                    pltpu.make_async_copy(
                        from_hbm[i].at[:, pl.ds(h * head, head)],
                        kv_prev.at[d - 1, i, h],
                        recv_sem.at[d - 1, i, h],
                    ).start()

    half = head // 2
    lane = lax.broadcasted_iota(jnp.int32, (1, head), 1)
    frequency = jnp.exp(
        lax.rem(lane, half).astype(jnp.float32) * (-2.0 * math.log(ROPE_BASE) / head)
    )
    sign = jnp.where(lane < half, -1.0, 1.0)

    targets = jnp.minimum(span, last - stretch)
    targets += (to_relay > 0).astype(jnp.int32) + (passed > 0).astype(jnp.int32)

    @pl.when(targets > 0)
    def _():
        pl.semaphore_wait(barrier, targets)

    each_by_relay(lambda copy: copy.start())

    @pl.when(uly == 1)
    def _():
        each_send(lambda copy: copy.start(), from_hbm)

    for copy in own_copies:
        copy.wait()

    @pl.when(uly == 0)
    def _():
        each_send(lambda copy: copy.start(), from_vmem)

    parts = angle_parts(stretch, rows, span, frequency)
    for copy in gain_copies:
        copy.wait()
    q_gain, k_gain = gains[0] * math.sqrt(head), gains[1] * math.sqrt(head)
    q_swap, k_swap = sign * pltpu.roll(q_gain, half, 1), sign * pltpu.roll(k_gain, half, 1)
    for d in range(span + 1):
        cosine, sine = rope_table(parts, d, rows)
        tab[d + 1, 0], tab[d + 1, 1] = cosine * k_gain, sine * k_swap
        if d == 0:
            tab[0, 0], tab[0, 1] = cosine * q_gain, sine * q_swap

    row = lax.broadcasted_iota(jnp.int32, (rows, rows), 0)
    col = lax.broadcasted_iota(jnp.int32, (rows, rows), 1)
    own = col <= row
    contract = (((1,), (1,)), ((), ()))
    from_lane = lax.broadcasted_iota(jnp.int32, (head, head), 0)
    to_lane = lax.broadcasted_iota(jnp.int32, (head, head), 1)
    swap = (from_lane == lax.rem(to_lane + half, head)).astype(jnp.float32)
    swap = swap.astype(jnp.bfloat16)

    for h in range(kv_heads):
        k_own[h] = rotate(
            kv_own[0, :, h * head : (h + 1) * head], tab[1, 0], tab[1, 1], swap
        )
        v_cat[h, :rows, :head] = kv_own[1, :, h * head : (h + 1) * head]
        v_cat[h, :, head:] = jnp.ones_like(v_cat[h, :, head:])
    for h in range(kv_heads):
        q_copies[h].wait()
        keys = k_own[h]
        for g in range(group):
            at = slice(g * rows, (g + 1) * rows)
            q_rot[h, at] = rotate(
                q_buf[h, :, g * head : (g + 1) * head], tab[0, 0], tab[0, 1], swap
            )
            scores = lax.dot_general(
                q_rot[h, at], keys, contract, preferred_element_type=jnp.float32
            )
            tiles[h, 0, at] = jnp.where(own, scores, NEG_FILL)

    scale = math.log2(math.e) / math.sqrt(head)
    keep = col <= row + jnp.where(stretch >= span, 0, rows)
    own_mask = own.astype(jnp.float32).astype(jnp.bfloat16)
    far_mask = 1.0 - own_mask
    bias = [
        jnp.where(stretch >= d, 0.0, NEG_FILL).astype(jnp.float32)
        for d in range(1, span)
    ]

    def arrived(h, i):
        for d in range(1, span + 1):
            remote(d, h, i, from_hbm[i]).wait_recv()

    def turn(h):
        for d in range(1, span + 1):
            k_far[h, (d - 1) * rows : d * rows] = rotate(
                kv_prev[d - 1, 0, h], tab[d + 1, 0], tab[d + 1, 1], swap
            )

    def score(h):
        for first in range(0, group, 4):
            at = slice(first * rows, (first + 4) * rows)
            scores = lax.dot_general(
                q_rot[h, at], k_far[h], contract, preferred_element_type=jnp.float32
            )
            tiles[h, 0, at] = jnp.where(
                jnp.concatenate([keep] * 4), tiles[h, 0, at], scores[:, (span - 1) * rows :]
            )
            for d in range(1, span):
                tiles[h, d, at] = scores[:, (d - 1) * rows : d * rows] + bias[d - 1]

    def weigh(h):
        for g in range(group):
            at = slice(g * rows, (g + 1) * rows)
            parts = [tiles[h, d, at] for d in range(span)]
            top = jnp.max(functools.reduce(jnp.maximum, parts), axis=-1, keepdims=True)
            for d in range(span):
                weights[h, d, at] = jnp.exp2((parts[d] - top) * scale).astype(jnp.bfloat16)

    def mix(h):
        for d in range(1, span + 1):
            v_cat[h, d * rows : (d + 1) * rows, :head] = kv_prev[d - 1, 1, h]
        values = v_cat[h]
        for first in range(0, group, 4):
            block = slice(first * rows, (first + 4) * rows)
            merged = weights[h, 0, block]
            spread = [merged * jnp.concatenate([own_mask] * 4)]
            spread += [weights[h, d, block] for d in range(1, span)]
            spread += [merged * jnp.concatenate([far_mask] * 4)]
            mixed = jnp.dot(
                jnp.concatenate(spread, axis=1), values, preferred_element_type=jnp.float32
            )
            for g in range(4):
                part = mixed[g * rows : (g + 1) * rows]
                at = h * width + (first + g) * head
                o_ref[:, at : at + head] = (part[:, :head] / part[:, head:]).astype(
                    o_ref.dtype
                )

    stages = [(0, lambda h: arrived(h, 0)), (0, turn), (1, score), (2, weigh)]
    stages += [(kv_heads, lambda h: arrived(h, 1)), (kv_heads, mix)]
    for step in range(-1, 2 * kv_heads):
        for lag, stage in stages:
            if 0 <= step - lag < kv_heads:
                stage(step - lag)
        for h in range(kv_heads):
            if step == h - 1:
                pass_on(h)

    each_by_relay(lambda copy: copy.wait_send())
    for h in range(kv_heads):

        @pl.when(h >= kv_heads - passed)
        def _(h=h):
            to_next_but_one(h).wait_send()

    @pl.when(uly == 1)
    def _():
        each_send(lambda copy: copy.wait_send(), from_hbm)

    @pl.when(uly == 0)
    def _():
        each_send(lambda copy: copy.wait_send(), from_vmem)


def in_hbm(array):
    return pltpu.with_memory_space_constraint(array, pltpu.HBM)


def local(query_proj, key_proj, value_projection, query_gain, key_gain):
    cycle = lax.axis_size("blk")
    span = max(1, cycle // 64)
    rows, head = query_proj.shape[0], query_gain.shape[0]
    kv_heads = key_proj.shape[1] // head
    group = query_proj.shape[1] // head // kv_heads
    bf16, f32 = jnp.bfloat16, jnp.float32
    vmem = pl.BlockSpec(memory_space=pltpu.VMEM)
    hbm = pl.BlockSpec(memory_space=pltpu.HBM)
    return pl.pallas_call(
        functools.partial(kernel, cycle, span, kv_heads, group),
        out_shape=jax.ShapeDtypeStruct(query_proj.shape, bf16),
        in_specs=[hbm] * 5,
        out_specs=vmem,
        scratch_shapes=[
            pltpu.VMEM((kv_heads, rows, group * head), bf16),
            pltpu.VMEM((2, rows, kv_heads * head), bf16),
            pltpu.VMEM((span, 2, kv_heads, rows, head), bf16),
            pltpu.VMEM((kv_heads, group * rows, head), bf16),
            pltpu.VMEM((kv_heads, rows, head), bf16),
            pltpu.VMEM((kv_heads, span * rows, head), bf16),
            pltpu.VMEM((kv_heads, (span + 1) * rows, 2 * head), bf16),
            pltpu.VMEM((kv_heads, span, group * rows, rows), f32),
            pltpu.VMEM((kv_heads, span, group * rows, rows), bf16),
            pltpu.VMEM((span + 2, 2, rows, head), f32),
            pltpu.VMEM((2, 1, head), f32),
            pltpu.VMEM((kv_heads, rows, head), bf16),
            pltpu.SemaphoreType.DMA((kv_heads,)),
            pltpu.SemaphoreType.DMA((2,)),
            pltpu.SemaphoreType.DMA((2,)),
            pltpu.SemaphoreType.DMA((span, 2, kv_heads)),
            pltpu.SemaphoreType.DMA((span, 2, kv_heads)),
            pltpu.SemaphoreType.DMA((kv_heads,)),
            pltpu.SemaphoreType.DMA((kv_heads,)),
        ],
        compiler_params=pltpu.CompilerParams(
            collective_id=0, has_side_effects=True, vmem_limit_bytes=24 * 1024 * 1024
        ),
        name="window_attention",
    )(
        in_hbm(query_proj),
        in_hbm(key_proj),
        in_hbm(value_projection),
        in_hbm(query_gain.reshape(1, head)),
        in_hbm(key_gain.reshape(1, head)),
    )


def solution(mesh):
    rows = P(("groups", "blk", "uly"), None)
    return jax.shard_map(
        local,
        mesh=mesh,
        in_specs=(rows, rows, rows, P(), P()),
        out_specs=rows,
        check_vma=False,
    )
```

```python
import functools
import math

import jax
import jax.numpy as jnp
from jax import lax
from jax.experimental import pallas as pl
from jax.experimental.pallas import tpu as pltpu
from jax.sharding import PartitionSpec as P

NEG_FILL = -1e30
ROPE_BASE = 1000000.0
EPS = 1e-06
MESH = pl.DeviceIdType.MESH


def angle_parts(stretch, rows, span, frequency):
    steps = rows // 8
    count = 8 + steps + 8 * pl.cdiv(span + 1, 8)
    index = lax.broadcasted_iota(jnp.int32, (count, frequency.shape[1]), 0)
    offset = jnp.where(
        index < 8,
        index,
        jnp.where(index < 8 + steps, (index - 8) * 8, (stretch - (index - 8 - steps)) * rows),
    )
    angle = offset.astype(jnp.float32) * frequency
    return jnp.cos(angle), jnp.sin(angle)


def rope_table(parts, d, rows):
    cosine, sine = parts
    steps = rows // 8
    fine_cos, fine_sin = cosine[:8], sine[:8]
    eights_cos, eights_sin = cosine[8 : 8 + steps], sine[8 : 8 + steps]
    at = 8 + steps + d
    first_cos, first_sin = cosine[at : at + 1], sine[at : at + 1]
    coarse_cos = eights_cos * first_cos - eights_sin * first_sin
    coarse_sin = eights_sin * first_cos + eights_cos * first_sin
    cosines, sines = [], []
    for j in range(steps):
        cos_j, sin_j = coarse_cos[j : j + 1], coarse_sin[j : j + 1]
        cosines.append(cos_j * fine_cos - sin_j * fine_sin)
        sines.append(sin_j * fine_cos + cos_j * fine_sin)
    return jnp.concatenate(cosines), jnp.concatenate(sines)


def rotate(x, table_a, table_b, swap):
    swapped = jnp.dot(x, swap, preferred_element_type=jnp.float32)
    x = x.astype(jnp.float32)
    r = lax.rsqrt(jnp.sum(x * x, axis=-1, keepdims=True) + x.shape[1] * EPS)
    return ((x * table_a + swapped * table_b) * r).astype(jnp.bfloat16)


def mix_head(weights, v_cat, o_ref, column, group, ready):
    span, rows, head = weights.shape[0], weights.shape[2], v_cat.shape[1] // 2
    row = lax.broadcasted_iota(jnp.int32, (rows, rows), 0)
    col = lax.broadcasted_iota(jnp.int32, (rows, rows), 1)
    own_mask = (col <= row).astype(jnp.float32).astype(jnp.bfloat16)
    far_mask = 1.0 - own_mask
    values = v_cat[...]
    half = max(1, group // 2)
    for part in range(group // half):
        block = slice(part * half * rows, (part + 1) * half * rows)
        merged = weights[0, block]
        spread = [merged * jnp.concatenate([own_mask] * half)]
        spread += [weights[d, block] for d in range(1, span)]
        spread += [merged * jnp.concatenate([far_mask] * half)]
        mixed = jnp.dot(
            jnp.concatenate(spread, axis=1), values, preferred_element_type=jnp.float32
        )
        for g in range(half):
            piece = mixed[g * rows : (g + 1) * rows]
            at = column + (part * half + g) * head
            o_ref[:, at : at + head] = (piece[:, :head] / piece[:, head:]).astype(
                o_ref.dtype
            )
        if ready is not None:
            ready(part)


def finish(group, o_most, w_last, v_last, o_hbm, o_last, sem):
    width = o_last.shape[1]
    copies = [
        pltpu.make_async_copy(
            o_most.at[:, pl.ds(h * width, width)],
            o_hbm.at[:, pl.ds(h * width, width)],
            sem.at[h],
        )
        for h in range(o_most.shape[1] // width)
    ]
    for copy in copies:
        copy.start()
    half = width // 2

    def ready(part):
        copy = pltpu.make_async_copy(
            o_last.at[:, pl.ds(part * half, half)],
            o_hbm.at[:, pl.ds(o_most.shape[1] + part * half, half)],
            sem.at[o_most.shape[1] // width + part],
        )
        copy.start()
        copies.append(copy)

    mix_head(w_last, v_last, o_last, 0, group, ready)
    for copy in copies:
        copy.wait()


def kernel(
    cycle, span, kv_heads, group,
    q_hbm, k_hbm, v_hbm, qg_hbm, kg_hbm, o_ref, w_last, v_last,
    q_buf, kv_own, kv_prev, q_rot, k_own, k_far, v_cat, tiles, weights, tab, gains,
    relay_buf, q_sem, own_sem, gain_sem, send_sem, recv_sem, pass_sem, relay_sem,
):
    rows, head = k_hbm.shape[0], qg_hbm.shape[1]
    width = group * head
    blk, uly = lax.axis_index("blk"), lax.axis_index("uly")
    last = 2 * cycle - 1
    stretch = jnp.where(uly == 0, blk, last - blk)

    def device_of(index):
        low = index < cycle
        return {"blk": jnp.where(low, index, last - index), "uly": jnp.where(low, 0, 1)}

    def relayed_by(index):
        some = (index >= cycle) & (index + 2 <= last) & (lax.rem(index, 2) == 0)
        return jnp.where(some, jnp.where(index == cycle, kv_heads, kv_heads - 1), 0)

    to_relay = jnp.where(stretch >= 1, relayed_by(stretch - 1), 0)
    passed = relayed_by(stretch)
    from_relay = jnp.where(stretch >= 2, relayed_by(stretch - 2), 0)

    barrier = pltpu.get_barrier_semaphore()

    def greet(index):
        pl.semaphore_signal(
            barrier, inc=1, device_id=device_of(index), device_id_type=MESH
        )

    for d in range(1, span + 1):
        pl.when(stretch >= d)(functools.partial(greet, stretch - d))
    pl.when(from_relay > 0)(functools.partial(greet, stretch - 2))
    pl.when(passed > 0)(functools.partial(greet, stretch + 1))

    own_copies = [
        pltpu.make_async_copy(src, kv_own.at[i], own_sem.at[i])
        for i, src in enumerate((k_hbm, v_hbm))
    ]
    q_copies = [
        pltpu.make_async_copy(
            q_hbm.at[:, pl.ds(h * width, width)], q_buf.at[h], q_sem.at[h]
        )
        for h in range(kv_heads)
    ]
    gain_copies = [
        pltpu.make_async_copy(src, gains.at[i], gain_sem.at[i])
        for i, src in enumerate((qg_hbm, kg_hbm))
    ]

    def remote(d, h, i, src):
        return pltpu.make_async_remote_copy(
            src_ref=src.at[:, pl.ds(h * head, head)],
            dst_ref=kv_prev.at[d - 1, i, h],
            send_sem=send_sem.at[d - 1, i, h],
            recv_sem=recv_sem.at[d - 1, i, h],
            device_id=device_of(stretch + d),
            device_id_type=MESH,
        )

    from_hbm = (k_hbm, v_hbm)
    from_vmem = (kv_own.at[0], kv_own.at[1])

    def each_send(act, sources):
        for i in range(2):
            for h in range(kv_heads):
                for d in range(1, span + 1):
                    sent = stretch + d <= last
                    if d == 1 and i == 1:
                        sent = sent & (h < kv_heads - to_relay)

                    @pl.when(sent)
                    def _(d=d, h=h, i=i):
                        act(remote(d, h, i, sources[i]))

    def to_next_but_one(h):
        return pltpu.make_async_remote_copy(
            src_ref=relay_buf.at[h],
            dst_ref=kv_prev.at[0, 1, h],
            send_sem=pass_sem.at[h],
            recv_sem=recv_sem.at[0, 1, h],
            device_id=device_of(stretch + 2),
            device_id_type=MESH,
        )

    def by_relay(h):
        return pltpu.make_async_remote_copy(
            src_ref=v_hbm.at[:, pl.ds(h * head, head)],
            dst_ref=relay_buf.at[h],
            send_sem=send_sem.at[0, 1, h],
            recv_sem=relay_sem.at[h],
            device_id=device_of(stretch - 1),
            device_id_type=MESH,
        )

    def each_by_relay(act):
        for h in range(kv_heads):

            @pl.when(h >= kv_heads - to_relay)
            def _(h=h):
                act(by_relay(h))

    def pass_on(h):
        @pl.when(h >= kv_heads - passed)
        def _():
            by_relay(h).wait_recv()
            to_next_but_one(h).start()

    for copy in own_copies + gain_copies + q_copies:
        copy.start()

    for d in range(1, span + 1):

        @pl.when(stretch < d)
        def _(d=d):
            for i in range(2):
                for h in range(kv_heads):
                    pltpu.make_async_copy(
                        from_hbm[i].at[:, pl.ds(h * head, head)],
                        kv_prev.at[d - 1, i, h],
                        recv_sem.at[d - 1, i, h],
                    ).start()

    half = head // 2
    lane = lax.broadcasted_iota(jnp.int32, (1, head), 1)
    frequency = jnp.exp(
        lax.rem(lane, half).astype(jnp.float32) * (-2.0 * math.log(ROPE_BASE) / head)
    )
    sign = jnp.where(lane < half, -1.0, 1.0)

    targets = jnp.minimum(span, last - stretch)
    targets += (to_relay > 0).astype(jnp.int32) + (passed > 0).astype(jnp.int32)

    @pl.when(targets > 0)
    def _():
        pl.semaphore_wait(barrier, targets)

    each_by_relay(lambda copy: copy.start())

    @pl.when(uly == 1)
    def _():
        each_send(lambda copy: copy.start(), from_hbm)

    for copy in own_copies:
        copy.wait()

    @pl.when(uly == 0)
    def _():
        each_send(lambda copy: copy.start(), from_vmem)

    parts = angle_parts(stretch, rows, span, frequency)
    for copy in gain_copies:
        copy.wait()
    q_gain, k_gain = gains[0] * math.sqrt(head), gains[1] * math.sqrt(head)
    q_swap, k_swap = sign * pltpu.roll(q_gain, half, 1), sign * pltpu.roll(k_gain, half, 1)
    for d in range(span + 1):
        cosine, sine = rope_table(parts, d, rows)
        tab[d + 1, 0], tab[d + 1, 1] = cosine * k_gain, sine * k_swap
        if d == 0:
            tab[0, 0], tab[0, 1] = cosine * q_gain, sine * q_swap

    row = lax.broadcasted_iota(jnp.int32, (rows, rows), 0)
    col = lax.broadcasted_iota(jnp.int32, (rows, rows), 1)
    own = col <= row
    contract = (((1,), (1,)), ((), ()))
    from_lane = lax.broadcasted_iota(jnp.int32, (head, head), 0)
    to_lane = lax.broadcasted_iota(jnp.int32, (head, head), 1)
    swap = (from_lane == lax.rem(to_lane + half, head)).astype(jnp.float32)
    swap = swap.astype(jnp.bfloat16)

    for h in range(kv_heads):
        k_own[h] = rotate(
            kv_own[0, :, h * head : (h + 1) * head], tab[1, 0], tab[1, 1], swap
        )
        values = v_last if h == kv_heads - 1 else v_cat.at[h]
        values[:rows, :head] = kv_own[1, :, h * head : (h + 1) * head]
        values[:, head:] = jnp.ones((values.shape[0], head), jnp.bfloat16)
    for h in range(kv_heads):
        q_copies[h].wait()
        keys = k_own[h]
        for g in range(group):
            at = slice(g * rows, (g + 1) * rows)
            q_rot[h, at] = rotate(
                q_buf[h, :, g * head : (g + 1) * head], tab[0, 0], tab[0, 1], swap
            )
            scores = lax.dot_general(
                q_rot[h, at], keys, contract, preferred_element_type=jnp.float32
            )
            tiles[h, 0, at] = jnp.where(own, scores, NEG_FILL)

    scale = math.log2(math.e) / math.sqrt(head)
    keep = col <= row + jnp.where(stretch >= span, 0, rows)
    bias = [
        jnp.where(stretch >= d, 0.0, NEG_FILL).astype(jnp.float32)
        for d in range(1, span)
    ]

    def arrived(h, i):
        for d in range(1, span + 1):
            remote(d, h, i, from_hbm[i]).wait_recv()

    def turn(h):
        for d in range(1, span + 1):
            k_far[h, (d - 1) * rows : d * rows] = rotate(
                kv_prev[d - 1, 0, h], tab[d + 1, 0], tab[d + 1, 1], swap
            )

    def score(h):
        for first in range(0, group, 4):
            at = slice(first * rows, (first + 4) * rows)
            scores = lax.dot_general(
                q_rot[h, at], k_far[h], contract, preferred_element_type=jnp.float32
            )
            tiles[h, 0, at] = jnp.where(
                jnp.concatenate([keep] * 4), tiles[h, 0, at], scores[:, (span - 1) * rows :]
            )
            for d in range(1, span):
                tiles[h, d, at] = scores[:, (d - 1) * rows : d * rows] + bias[d - 1]

    def weigh(h):
        for g in range(group):
            at = slice(g * rows, (g + 1) * rows)
            parts = [tiles[h, d, at] for d in range(span)]
            top = jnp.max(functools.reduce(jnp.maximum, parts), axis=-1, keepdims=True)
            for d in range(span):
                out = w_last if h == kv_heads - 1 else weights.at[h]
                out[d, at] = jnp.exp2((parts[d] - top) * scale).astype(jnp.bfloat16)

    def join(h):
        values = v_last if h == kv_heads - 1 else v_cat.at[h]
        for d in range(1, span + 1):
            values[d * rows : (d + 1) * rows, :head] = kv_prev[d - 1, 1, h]

    def mix(h):
        if h < kv_heads - 1:
            join(h)
            mix_head(weights.at[h], v_cat.at[h], o_ref, h * width, group, None)

    stages = [(0, lambda h: arrived(h, 0)), (0, turn), (1, score), (2, weigh)]
    stages += [(kv_heads, lambda h: arrived(h, 1)), (kv_heads, mix)]
    for step in range(-1, 2 * kv_heads):
        for lag, stage in stages:
            if 0 <= step - lag < kv_heads:
                stage(step - lag)
        for h in range(kv_heads):
            if step == h - 1:
                pass_on(h)
    join(kv_heads - 1)

    each_by_relay(lambda copy: copy.wait_send())
    for h in range(kv_heads):

        @pl.when(h >= kv_heads - passed)
        def _(h=h):
            to_next_but_one(h).wait_send()

    @pl.when(uly == 1)
    def _():
        each_send(lambda copy: copy.wait_send(), from_hbm)

    @pl.when(uly == 0)
    def _():
        each_send(lambda copy: copy.wait_send(), from_vmem)


def in_hbm(array):
    return pltpu.with_memory_space_constraint(array, pltpu.HBM)


def local(query_proj, key_proj, value_projection, query_gain, key_gain):
    cycle = lax.axis_size("blk")
    span = max(1, cycle // 64)
    rows, head = query_proj.shape[0], query_gain.shape[0]
    kv_heads = key_proj.shape[1] // head
    group = query_proj.shape[1] // head // kv_heads
    bf16, f32 = jnp.bfloat16, jnp.float32
    vmem = pl.BlockSpec(memory_space=pltpu.VMEM)
    hbm = pl.BlockSpec(memory_space=pltpu.HBM)
    most = (kv_heads - 1) * group * head
    o_most, w_last, v_last = pl.pallas_call(
        functools.partial(kernel, cycle, span, kv_heads, group),
        out_shape=[
            jax.ShapeDtypeStruct((rows, most), bf16),
            jax.ShapeDtypeStruct((span, group * rows, rows), bf16),
            jax.ShapeDtypeStruct(((span + 1) * rows, 2 * head), bf16),
        ],
        in_specs=[hbm] * 5,
        out_specs=[vmem] * 3,
        scratch_shapes=[
            pltpu.VMEM((kv_heads, rows, group * head), bf16),
            pltpu.VMEM((2, rows, kv_heads * head), bf16),
            pltpu.VMEM((span, 2, kv_heads, rows, head), bf16),
            pltpu.VMEM((kv_heads, group * rows, head), bf16),
            pltpu.VMEM((kv_heads, rows, head), bf16),
            pltpu.VMEM((kv_heads, span * rows, head), bf16),
            pltpu.VMEM((kv_heads, (span + 1) * rows, 2 * head), bf16),
            pltpu.VMEM((kv_heads, span, group * rows, rows), f32),
            pltpu.VMEM((kv_heads, span, group * rows, rows), bf16),
            pltpu.VMEM((span + 2, 2, rows, head), f32),
            pltpu.VMEM((2, 1, head), f32),
            pltpu.VMEM((kv_heads, rows, head), bf16),
            pltpu.SemaphoreType.DMA((kv_heads,)),
            pltpu.SemaphoreType.DMA((2,)),
            pltpu.SemaphoreType.DMA((2,)),
            pltpu.SemaphoreType.DMA((span, 2, kv_heads)),
            pltpu.SemaphoreType.DMA((span, 2, kv_heads)),
            pltpu.SemaphoreType.DMA((kv_heads,)),
            pltpu.SemaphoreType.DMA((kv_heads,)),
        ],
        compiler_params=pltpu.CompilerParams(
            collective_id=0, has_side_effects=True, vmem_limit_bytes=24 * 1024 * 1024
        ),
        name="window_attention",
    )(
        in_hbm(query_proj),
        in_hbm(key_proj),
        in_hbm(value_projection),
        in_hbm(query_gain.reshape(1, head)),
        in_hbm(key_gain.reshape(1, head)),
    )
    return pl.pallas_call(
        functools.partial(finish, group),
        out_shape=jax.ShapeDtypeStruct(query_proj.shape, bf16),
        in_specs=[vmem] * 3,
        out_specs=hbm,
        scratch_shapes=[
            pltpu.VMEM((rows, group * head), bf16),
            pltpu.SemaphoreType.DMA((kv_heads + 1,)),
        ],
        compiler_params=pltpu.CompilerParams(vmem_limit_bytes=8 * 1024 * 1024),
        name="last_heads",
    )(o_most, w_last, v_last)


def solution(mesh):
    rows = P(("groups", "blk", "uly"), None)
    return jax.shard_map(
        local,
        mesh=mesh,
        in_specs=(rows, rows, rows, P(), P()),
        out_specs=rows,
        check_vma=False,
    )
```

```python
import functools
import math

import jax
import jax.numpy as jnp
from jax import lax
from jax.experimental import pallas as pl
from jax.experimental.pallas import tpu as pltpu
from jax.sharding import PartitionSpec as P

NEG_FILL = -1e30
ROPE_BASE = 1000000.0
EPS = 1e-06
MESH = pl.DeviceIdType.MESH


def angle_parts(stretch, rows, span, frequency):
    steps = rows // 8
    count = 8 + steps + 8 * pl.cdiv(span + 1, 8)
    index = lax.broadcasted_iota(jnp.int32, (count, frequency.shape[1]), 0)
    offset = jnp.where(
        index < 8,
        index,
        jnp.where(index < 8 + steps, (index - 8) * 8, (stretch - (index - 8 - steps)) * rows),
    )
    angle = offset.astype(jnp.float32) * frequency
    return jnp.cos(angle), jnp.sin(angle)


def rope_table(parts, d, rows):
    cosine, sine = parts
    steps = rows // 8
    fine_cos, fine_sin = cosine[:8], sine[:8]
    eights_cos, eights_sin = cosine[8 : 8 + steps], sine[8 : 8 + steps]
    at = 8 + steps + d
    first_cos, first_sin = cosine[at : at + 1], sine[at : at + 1]
    coarse_cos = eights_cos * first_cos - eights_sin * first_sin
    coarse_sin = eights_sin * first_cos + eights_cos * first_sin
    cosines, sines = [], []
    for j in range(steps):
        cos_j, sin_j = coarse_cos[j : j + 1], coarse_sin[j : j + 1]
        cosines.append(cos_j * fine_cos - sin_j * fine_sin)
        sines.append(sin_j * fine_cos + cos_j * fine_sin)
    return jnp.concatenate(cosines), jnp.concatenate(sines)


def rotate(x, table_a, table_b, swap):
    swapped = jnp.dot(x, swap, preferred_element_type=jnp.float32)
    x = x.astype(jnp.float32)
    r = lax.rsqrt(jnp.sum(x * x, axis=-1, keepdims=True) + x.shape[1] * EPS)
    return ((x * table_a + swapped * table_b) * r).astype(jnp.bfloat16)


def mix_head(weights, v_cat, o_ref, column, group, ready):
    span, rows, head = weights.shape[0], weights.shape[2], v_cat.shape[1] // 2
    row = lax.broadcasted_iota(jnp.int32, (rows, rows), 0)
    col = lax.broadcasted_iota(jnp.int32, (rows, rows), 1)
    own_mask = (col <= row).astype(jnp.float32).astype(jnp.bfloat16)
    far_mask = 1.0 - own_mask
    values = v_cat[...]
    half = max(1, group // 2)
    for part in range(group // half):
        block = slice(part * half * rows, (part + 1) * half * rows)
        merged = weights[0, block]
        spread = [merged * jnp.concatenate([own_mask] * half)]
        spread += [weights[d, block] for d in range(1, span)]
        spread += [merged * jnp.concatenate([far_mask] * half)]
        mixed = jnp.dot(
            jnp.concatenate(spread, axis=1), values, preferred_element_type=jnp.float32
        )
        for g in range(half):
            piece = mixed[g * rows : (g + 1) * rows]
            at = column + (part * half + g) * head
            o_ref[:, at : at + head] = (piece[:, :head] / piece[:, head:]).astype(
                o_ref.dtype
            )
        if ready is not None:
            ready(part)


def finish(group, o_most, w_last, v_last, o_hbm, o_last, sem):
    width = o_last.shape[1]
    copies = [
        pltpu.make_async_copy(
            o_most.at[:, pl.ds(h * width, width)],
            o_hbm.at[:, pl.ds(h * width, width)],
            sem.at[h],
        )
        for h in range(o_most.shape[1] // width)
    ]
    for copy in copies:
        copy.start()
    half = width // 2

    def ready(part):
        copy = pltpu.make_async_copy(
            o_last.at[:, pl.ds(part * half, half)],
            o_hbm.at[:, pl.ds(o_most.shape[1] + part * half, half)],
            sem.at[o_most.shape[1] // width + part],
        )
        copy.start()
        copies.append(copy)

    mix_head(w_last, v_last, o_last, 0, group, ready)
    for copy in copies:
        copy.wait()


def kernel(
    cycle, span, kv_heads, group,
    q_hbm, k_hbm, v_hbm, qg_hbm, kg_hbm, o_ref, w_last, v_last,
    q_buf, kv_own, kv_prev, q_rot, k_own, k_far, v_cat, tiles, weights, tab, gains,
    relay_buf, q_sem, own_sem, gain_sem, send_sem, recv_sem, pass_sem, relay_sem,
):
    rows, head = k_hbm.shape[0], qg_hbm.shape[1]
    width = group * head
    blk, uly = lax.axis_index("blk"), lax.axis_index("uly")
    last = 2 * cycle - 1
    stretch = jnp.where(uly == 0, blk, last - blk)

    def device_of(index):
        low = index < cycle
        return {"blk": jnp.where(low, index, last - index), "uly": jnp.where(low, 0, 1)}

    def count_between(relay):
        high = (relay >= cycle) & (relay + 2 <= last) & (lax.rem(relay, 2) == 0)
        return jnp.where(high, kv_heads - 1, jnp.where(relay == 2, kv_heads - 1, 0))

    relay = jnp.where(stretch == 0, 2, jnp.maximum(stretch - 1, 0))
    odd = (lax.rem(stretch, 2) == 1) & (stretch > cycle)
    to_relay = jnp.where(odd | (stretch == 0), count_between(relay), 0)
    passed = count_between(stretch)
    source = jnp.where(stretch == 2, 0, jnp.minimum(stretch + 1, last))
    target = jnp.where(stretch == 2, 1, jnp.minimum(stretch + 2, last))
    passer = jnp.where(stretch == 1, 2, jnp.maximum(stretch - 2, 0))
    fed = (stretch == 1) | ((lax.rem(stretch, 2) == 0) & (stretch > cycle + 1))
    from_relay = jnp.where(fed, count_between(passer), 0)

    barrier = pltpu.get_barrier_semaphore()

    def greet(index):
        pl.semaphore_signal(
            barrier, inc=1, device_id=device_of(index), device_id_type=MESH
        )

    for d in range(1, span + 1):
        pl.when(stretch >= d)(functools.partial(greet, stretch - d))
    pl.when(from_relay > 0)(functools.partial(greet, passer))
    pl.when(passed > 0)(functools.partial(greet, source))

    own_copies = [
        pltpu.make_async_copy(src, kv_own.at[i], own_sem.at[i])
        for i, src in enumerate((k_hbm, v_hbm))
    ]
    q_copies = [
        pltpu.make_async_copy(
            q_hbm.at[:, pl.ds(h * width, width)], q_buf.at[h], q_sem.at[h]
        )
        for h in range(kv_heads)
    ]
    gain_copies = [
        pltpu.make_async_copy(src, gains.at[i], gain_sem.at[i])
        for i, src in enumerate((qg_hbm, kg_hbm))
    ]

    def remote(d, h, i, src):
        return pltpu.make_async_remote_copy(
            src_ref=src.at[:, pl.ds(h * head, head)],
            dst_ref=kv_prev.at[d - 1, i, h],
            send_sem=send_sem.at[d - 1, i, h],
            recv_sem=recv_sem.at[d - 1, i, h],
            device_id=device_of(stretch + d),
            device_id_type=MESH,
        )

    from_hbm = (k_hbm, v_hbm)
    from_vmem = (kv_own.at[0], kv_own.at[1])

    def each_send(act, sources):
        for i in range(2):
            for h in range(kv_heads):
                for d in range(1, span + 1):
                    sent = stretch + d <= last
                    if d == 1 and i == 1:
                        sent = sent & (h < kv_heads - to_relay)

                    @pl.when(sent)
                    def _(d=d, h=h, i=i):
                        act(remote(d, h, i, sources[i]))

    def to_target(h):
        return pltpu.make_async_remote_copy(
            src_ref=relay_buf.at[h],
            dst_ref=kv_prev.at[0, 1, h],
            send_sem=pass_sem.at[h],
            recv_sem=recv_sem.at[0, 1, h],
            device_id=device_of(target),
            device_id_type=MESH,
        )

    def by_relay(h):
        return pltpu.make_async_remote_copy(
            src_ref=v_hbm.at[:, pl.ds(h * head, head)],
            dst_ref=relay_buf.at[h],
            send_sem=send_sem.at[0, 1, h],
            recv_sem=relay_sem.at[h],
            device_id=device_of(relay),
            device_id_type=MESH,
        )

    def each_by_relay(act):
        for h in range(kv_heads):

            @pl.when(h >= kv_heads - to_relay)
            def _(h=h):
                act(by_relay(h))

    def pass_on(h, when):
        @pl.when(when & (h >= kv_heads - passed))
        def _():
            by_relay(h).wait_recv()
            to_target(h).start()

    for copy in own_copies + gain_copies + q_copies:
        copy.start()

    for d in range(1, span + 1):

        @pl.when(stretch < d)
        def _(d=d):
            for i in range(2):
                for h in range(kv_heads):
                    pltpu.make_async_copy(
                        from_hbm[i].at[:, pl.ds(h * head, head)],
                        kv_prev.at[d - 1, i, h],
                        recv_sem.at[d - 1, i, h],
                    ).start()

    half = head // 2
    lane = lax.broadcasted_iota(jnp.int32, (1, head), 1)
    frequency = jnp.exp(
        lax.rem(lane, half).astype(jnp.float32) * (-2.0 * math.log(ROPE_BASE) / head)
    )
    sign = jnp.where(lane < half, -1.0, 1.0)

    targets = jnp.minimum(span, last - stretch)
    targets += (to_relay > 0).astype(jnp.int32) + (passed > 0).astype(jnp.int32)

    def wait_for_targets():
        @pl.when(targets > 0)
        def _():
            pl.semaphore_wait(barrier, targets)

        each_by_relay(lambda copy: copy.start())

    pl.when(stretch > 0)(wait_for_targets)

    @pl.when((uly == 1) & (to_relay == 0))
    def _():
        each_send(lambda copy: copy.start(), from_hbm)

    for copy in own_copies:
        copy.wait()

    @pl.when((uly == 0) & (stretch > 0))
    def _():
        each_send(lambda copy: copy.start(), from_vmem)

    parts = angle_parts(stretch, rows, span, frequency)
    for copy in gain_copies:
        copy.wait()
    q_gain, k_gain = gains[0] * math.sqrt(head), gains[1] * math.sqrt(head)
    q_swap, k_swap = sign * pltpu.roll(q_gain, half, 1), sign * pltpu.roll(k_gain, half, 1)
    for d in range(span + 1):
        cosine, sine = rope_table(parts, d, rows)
        tab[d + 1, 0], tab[d + 1, 1] = cosine * k_gain, sine * k_swap
        if d == 0:
            tab[0, 0], tab[0, 1] = cosine * q_gain, sine * q_swap

    row = lax.broadcasted_iota(jnp.int32, (rows, rows), 0)
    col = lax.broadcasted_iota(jnp.int32, (rows, rows), 1)
    own = col <= row
    contract = (((1,), (1,)), ((), ()))
    from_lane = lax.broadcasted_iota(jnp.int32, (head, head), 0)
    to_lane = lax.broadcasted_iota(jnp.int32, (head, head), 1)
    swap = (from_lane == lax.rem(to_lane + half, head)).astype(jnp.float32)
    swap = swap.astype(jnp.bfloat16)

    for h in range(kv_heads):
        k_own[h] = rotate(
            kv_own[0, :, h * head : (h + 1) * head], tab[1, 0], tab[1, 1], swap
        )
        values = v_last if h == kv_heads - 1 else v_cat.at[h]
        values[:rows, :head] = kv_own[1, :, h * head : (h + 1) * head]
        values[:, head:] = jnp.ones((values.shape[0], head), jnp.bfloat16)
    for h in range(kv_heads):
        if h == 0:

            @pl.when(stretch == 0)
            def _():
                wait_for_targets()
                each_send(lambda copy: copy.start(), from_vmem)

        if h == kv_heads - 1:
            for late in range(kv_heads):
                pass_on(late, stretch == 2)
        q_copies[h].wait()
        keys = k_own[h]
        for g in range(group):
            if h == 0 and g == 0:

                @pl.when((uly == 1) & (to_relay > 0))
                def _():
                    each_send(lambda copy: copy.start(), from_hbm)

            at = slice(g * rows, (g + 1) * rows)
            q_rot[h, at] = rotate(
                q_buf[h, :, g * head : (g + 1) * head], tab[0, 0], tab[0, 1], swap
            )
            scores = lax.dot_general(
                q_rot[h, at], keys, contract, preferred_element_type=jnp.float32
            )
            tiles[h, 0, at] = jnp.where(own, scores, NEG_FILL)

    scale = math.log2(math.e) / math.sqrt(head)
    keep = col <= row + jnp.where(stretch >= span, 0, rows)
    bias = [
        jnp.where(stretch >= d, 0.0, NEG_FILL).astype(jnp.float32)
        for d in range(1, span)
    ]

    def arrived(h, i):
        for d in range(1, span + 1):
            remote(d, h, i, from_hbm[i]).wait_recv()

    def turn(h):
        for d in range(1, span + 1):
            k_far[h, (d - 1) * rows : d * rows] = rotate(
                kv_prev[d - 1, 0, h], tab[d + 1, 0], tab[d + 1, 1], swap
            )

    def score(h):
        for first in range(0, group, 4):
            at = slice(first * rows, (first + 4) * rows)
            scores = lax.dot_general(
                q_rot[h, at], k_far[h], contract, preferred_element_type=jnp.float32
            )
            tiles[h, 0, at] = jnp.where(
                jnp.concatenate([keep] * 4), tiles[h, 0, at], scores[:, (span - 1) * rows :]
            )
            for d in range(1, span):
                tiles[h, d, at] = scores[:, (d - 1) * rows : d * rows] + bias[d - 1]

    def weigh(h):
        for g in range(group):
            at = slice(g * rows, (g + 1) * rows)
            parts = [tiles[h, d, at] for d in range(span)]
            top = jnp.max(functools.reduce(jnp.maximum, parts), axis=-1, keepdims=True)
            for d in range(span):
                out = w_last if h == kv_heads - 1 else weights.at[h]
                out[d, at] = jnp.exp2((parts[d] - top) * scale).astype(jnp.bfloat16)

    def join(h):
        values = v_last if h == kv_heads - 1 else v_cat.at[h]
        for d in range(1, span + 1):
            values[d * rows : (d + 1) * rows, :head] = kv_prev[d - 1, 1, h]

    def mix(h):
        if h < kv_heads - 1:
            join(h)
            mix_head(weights.at[h], v_cat.at[h], o_ref, h * width, group, None)

    stages = [(0, lambda h: arrived(h, 0)), (0, turn), (1, score), (2, weigh)]
    stages += [(kv_heads, lambda h: arrived(h, 1)), (kv_heads, mix)]
    for step in range(-1, 2 * kv_heads):
        for lag, stage in stages:
            if 0 <= step - lag < kv_heads:
                stage(step - lag)
        for h in range(kv_heads):
            if step == -1:
                pass_on(h, stretch != 2)
    join(kv_heads - 1)

    each_by_relay(lambda copy: copy.wait_send())
    for h in range(kv_heads):

        @pl.when(h >= kv_heads - passed)
        def _(h=h):
            to_target(h).wait_send()

    @pl.when(uly == 1)
    def _():
        each_send(lambda copy: copy.wait_send(), from_hbm)

    @pl.when(uly == 0)
    def _():
        each_send(lambda copy: copy.wait_send(), from_vmem)


def in_hbm(array):
    return pltpu.with_memory_space_constraint(array, pltpu.HBM)


def local(query_proj, key_proj, value_projection, query_gain, key_gain):
    cycle = lax.axis_size("blk")
    span = max(1, cycle // 64)
    rows, head = query_proj.shape[0], query_gain.shape[0]
    kv_heads = key_proj.shape[1] // head
    group = query_proj.shape[1] // head // kv_heads
    bf16, f32 = jnp.bfloat16, jnp.float32
    vmem = pl.BlockSpec(memory_space=pltpu.VMEM)
    hbm = pl.BlockSpec(memory_space=pltpu.HBM)
    most = (kv_heads - 1) * group * head
    o_most, w_last, v_last = pl.pallas_call(
        functools.partial(kernel, cycle, span, kv_heads, group),
        out_shape=[
            jax.ShapeDtypeStruct((rows, most), bf16),
            jax.ShapeDtypeStruct((span, group * rows, rows), bf16),
            jax.ShapeDtypeStruct(((span + 1) * rows, 2 * head), bf16),
        ],
        in_specs=[hbm] * 5,
        out_specs=[vmem] * 3,
        scratch_shapes=[
            pltpu.VMEM((kv_heads, rows, group * head), bf16),
            pltpu.VMEM((2, rows, kv_heads * head), bf16),
            pltpu.VMEM((span, 2, kv_heads, rows, head), bf16),
            pltpu.VMEM((kv_heads, group * rows, head), bf16),
            pltpu.VMEM((kv_heads, rows, head), bf16),
            pltpu.VMEM((kv_heads, span * rows, head), bf16),
            pltpu.VMEM((kv_heads, (span + 1) * rows, 2 * head), bf16),
            pltpu.VMEM((kv_heads, span, group * rows, rows), f32),
            pltpu.VMEM((kv_heads, span, group * rows, rows), bf16),
            pltpu.VMEM((span + 2, 2, rows, head), f32),
            pltpu.VMEM((2, 1, head), f32),
            pltpu.VMEM((kv_heads, rows, head), bf16),
            pltpu.SemaphoreType.DMA((kv_heads,)),
            pltpu.SemaphoreType.DMA((2,)),
            pltpu.SemaphoreType.DMA((2,)),
            pltpu.SemaphoreType.DMA((span, 2, kv_heads)),
            pltpu.SemaphoreType.DMA((span, 2, kv_heads)),
            pltpu.SemaphoreType.DMA((kv_heads,)),
            pltpu.SemaphoreType.DMA((kv_heads,)),
        ],
        compiler_params=pltpu.CompilerParams(
            collective_id=0, has_side_effects=True, vmem_limit_bytes=24 * 1024 * 1024
        ),
        name="window_attention",
    )(
        in_hbm(query_proj),
        in_hbm(key_proj),
        in_hbm(value_projection),
        in_hbm(query_gain.reshape(1, head)),
        in_hbm(key_gain.reshape(1, head)),
    )
    return pl.pallas_call(
        functools.partial(finish, group),
        out_shape=jax.ShapeDtypeStruct(query_proj.shape, bf16),
        in_specs=[vmem] * 3,
        out_specs=hbm,
        scratch_shapes=[
            pltpu.VMEM((rows, group * head), bf16),
            pltpu.SemaphoreType.DMA((kv_heads + 1,)),
        ],
        compiler_params=pltpu.CompilerParams(vmem_limit_bytes=8 * 1024 * 1024),
        name="last_heads",
    )(o_most, w_last, v_last)


def solution(mesh):
    rows = P(("groups", "blk", "uly"), None)
    return jax.shard_map(
        local,
        mesh=mesh,
        in_specs=(rows, rows, rows, P(), P()),
        out_specs=rows,
        check_vma=False,
    )
```

```python
import functools
import math

import jax
import jax.numpy as jnp
from jax import lax
from jax.experimental import pallas as pl
from jax.experimental.pallas import tpu as pltpu
from jax.sharding import PartitionSpec as P

NEG_FILL = -1e30
ROPE_BASE = 1000000.0
EPS = 1e-06
MESH = pl.DeviceIdType.MESH


def angle_parts(stretch, rows, span, frequency):
    steps = rows // 8
    count = 8 + steps + 8 * pl.cdiv(span + 1, 8)
    index = lax.broadcasted_iota(jnp.int32, (count, frequency.shape[1]), 0)
    offset = jnp.where(
        index < 8,
        index,
        jnp.where(index < 8 + steps, (index - 8) * 8, (stretch - (index - 8 - steps)) * rows),
    )
    angle = offset.astype(jnp.float32) * frequency
    return jnp.cos(angle), jnp.sin(angle)


def rope_table(parts, d, rows):
    cosine, sine = parts
    steps = rows // 8
    fine_cos, fine_sin = cosine[:8], sine[:8]
    eights_cos, eights_sin = cosine[8 : 8 + steps], sine[8 : 8 + steps]
    at = 8 + steps + d
    first_cos, first_sin = cosine[at : at + 1], sine[at : at + 1]
    coarse_cos = eights_cos * first_cos - eights_sin * first_sin
    coarse_sin = eights_sin * first_cos + eights_cos * first_sin
    cosines, sines = [], []
    for j in range(steps):
        cos_j, sin_j = coarse_cos[j : j + 1], coarse_sin[j : j + 1]
        cosines.append(cos_j * fine_cos - sin_j * fine_sin)
        sines.append(sin_j * fine_cos + cos_j * fine_sin)
    return jnp.concatenate(cosines), jnp.concatenate(sines)


def rotate(x, table_a, table_b, swap):
    swapped = jnp.dot(x, swap, preferred_element_type=jnp.float32)
    x = x.astype(jnp.float32)
    r = lax.rsqrt(jnp.sum(x * x, axis=-1, keepdims=True) + x.shape[1] * EPS)
    return ((x * table_a + swapped * table_b) * r).astype(jnp.bfloat16)


def mix_head(weights, v_cat, o_ref, column, group, ready):
    span, rows, head = weights.shape[0], weights.shape[2], v_cat.shape[1] // 2
    row = lax.broadcasted_iota(jnp.int32, (rows, rows), 0)
    col = lax.broadcasted_iota(jnp.int32, (rows, rows), 1)
    own_mask = (col <= row).astype(jnp.float32).astype(jnp.bfloat16)
    far_mask = 1.0 - own_mask
    values = v_cat[...]
    half = max(1, group // 2)
    for part in range(group // half):
        block = slice(part * half * rows, (part + 1) * half * rows)
        merged = weights[0, block]
        spread = [merged * jnp.concatenate([own_mask] * half)]
        spread += [weights[d, block] for d in range(1, span)]
        spread += [merged * jnp.concatenate([far_mask] * half)]
        mixed = jnp.dot(
            jnp.concatenate(spread, axis=1), values, preferred_element_type=jnp.float32
        )
        for g in range(half):
            piece = mixed[g * rows : (g + 1) * rows]
            at = column + (part * half + g) * head
            o_ref[:, at : at + head] = (piece[:, :head] / piece[:, head:]).astype(
                o_ref.dtype
            )
        if ready is not None:
            ready(part)


def finish(group, o_most, w_last, v_last, o_hbm, o_last, sem):
    width, most = o_last.shape[1], o_most.shape[1]
    copies = [pltpu.make_async_copy(o_most, o_hbm.at[:, pl.ds(0, most)], sem.at[0])]
    copies[0].start()
    half = width // 2

    def ready(part):
        copy = pltpu.make_async_copy(
            o_last.at[:, pl.ds(part * half, half)],
            o_hbm.at[:, pl.ds(most + part * half, half)],
            sem.at[1 + part],
        )
        copy.start()
        copies.append(copy)

    mix_head(w_last, v_last, o_last, 0, group, ready)
    for copy in copies:
        copy.wait()


def kernel(
    cycle, span, kv_heads, group,
    q_hbm, k_hbm, v_hbm, qg_hbm, kg_hbm, o_ref, w_last, v_last,
    q_buf, kv_own, kv_prev, q_rot, k_own, k_far, v_cat, tiles, weights, tab, gains,
    relay_buf, q_sem, own_sem, gain_sem, send_sem, recv_sem, pass_sem, relay_sem,
):
    rows, head = k_hbm.shape[0], qg_hbm.shape[1]
    width = group * head
    blk, uly = lax.axis_index("blk"), lax.axis_index("uly")
    last = 2 * cycle - 1
    stretch = jnp.where(uly == 0, blk, last - blk)

    def device_of(index):
        low = index < cycle
        return {"blk": jnp.where(low, index, last - index), "uly": jnp.where(low, 0, 1)}

    def count_between(relay):
        high = (relay >= cycle) & (relay + 2 <= last) & (lax.rem(relay, 2) == 0)
        return jnp.where(high, kv_heads - 1, jnp.where(relay == 2, kv_heads - 1, 0))

    relay = jnp.where(stretch == 0, 2, jnp.maximum(stretch - 1, 0))
    odd = (lax.rem(stretch, 2) == 1) & (stretch > cycle)
    to_relay = jnp.where(odd | (stretch == 0), count_between(relay), 0)
    passed = count_between(stretch)
    source = jnp.where(stretch == 2, 0, jnp.minimum(stretch + 1, last))
    target = jnp.where(stretch == 2, 1, jnp.minimum(stretch + 2, last))
    passer = jnp.where(stretch == 1, 2, jnp.maximum(stretch - 2, 0))
    fed = (stretch == 1) | ((lax.rem(stretch, 2) == 0) & (stretch > cycle + 1))
    from_relay = jnp.where(fed, count_between(passer), 0)

    barrier = pltpu.get_barrier_semaphore()

    def greet(index):
        pl.semaphore_signal(
            barrier, inc=1, device_id=device_of(index), device_id_type=MESH
        )

    for d in range(1, span + 1):
        pl.when(stretch >= d)(functools.partial(greet, stretch - d))
    pl.when(from_relay > 0)(functools.partial(greet, passer))
    pl.when(passed > 0)(functools.partial(greet, source))

    own_copies = [
        pltpu.make_async_copy(src, kv_own.at[i], own_sem.at[i])
        for i, src in enumerate((k_hbm, v_hbm))
    ]
    q_copies = [
        pltpu.make_async_copy(
            q_hbm.at[:, pl.ds(h * width, width)], q_buf.at[h], q_sem.at[h]
        )
        for h in range(kv_heads)
    ]
    gain_copies = [
        pltpu.make_async_copy(src, gains.at[i], gain_sem.at[i])
        for i, src in enumerate((qg_hbm, kg_hbm))
    ]

    def remote(d, h, i, src):
        return pltpu.make_async_remote_copy(
            src_ref=src.at[:, pl.ds(h * head, head)],
            dst_ref=kv_prev.at[d - 1, i, h],
            send_sem=send_sem.at[d - 1, i, h],
            recv_sem=recv_sem.at[d - 1, i, h],
            device_id=device_of(stretch + d),
            device_id_type=MESH,
        )

    from_hbm = (k_hbm, v_hbm)
    from_vmem = (kv_own.at[0], kv_own.at[1])

    def each_send(act, sources):
        for i in range(2):
            for h in range(kv_heads):
                for d in range(1, span + 1):
                    sent = stretch + d <= last
                    if d == 1 and i == 1:
                        sent = sent & (h < kv_heads - to_relay)

                    @pl.when(sent)
                    def _(d=d, h=h, i=i):
                        act(remote(d, h, i, sources[i]))

    def to_target(h):
        return pltpu.make_async_remote_copy(
            src_ref=relay_buf.at[h],
            dst_ref=kv_prev.at[0, 1, h],
            send_sem=pass_sem.at[h],
            recv_sem=recv_sem.at[0, 1, h],
            device_id=device_of(target),
            device_id_type=MESH,
        )

    def by_relay(h):
        return pltpu.make_async_remote_copy(
            src_ref=v_hbm.at[:, pl.ds(h * head, head)],
            dst_ref=relay_buf.at[h],
            send_sem=send_sem.at[0, 1, h],
            recv_sem=relay_sem.at[h],
            device_id=device_of(relay),
            device_id_type=MESH,
        )

    def each_by_relay(act):
        for h in range(kv_heads):

            @pl.when(h >= kv_heads - to_relay)
            def _(h=h):
                act(by_relay(h))

    def pass_on(h, when):
        @pl.when(when & (h >= kv_heads - passed))
        def _():
            by_relay(h).wait_recv()
            to_target(h).start()

    for copy in own_copies + gain_copies + q_copies:
        copy.start()

    for d in range(1, span + 1):

        @pl.when(stretch < d)
        def _(d=d):
            for i in range(2):
                for h in range(kv_heads):
                    pltpu.make_async_copy(
                        from_hbm[i].at[:, pl.ds(h * head, head)],
                        kv_prev.at[d - 1, i, h],
                        recv_sem.at[d - 1, i, h],
                    ).start()

    half = head // 2
    lane = lax.broadcasted_iota(jnp.int32, (1, head), 1)
    frequency = jnp.exp(
        lax.rem(lane, half).astype(jnp.float32) * (-2.0 * math.log(ROPE_BASE) / head)
    )
    sign = jnp.where(lane < half, -1.0, 1.0)

    targets = jnp.minimum(span, last - stretch)
    targets += (to_relay > 0).astype(jnp.int32) + (passed > 0).astype(jnp.int32)

    def wait_for_targets():
        @pl.when(targets > 0)
        def _():
            pl.semaphore_wait(barrier, targets)

        each_by_relay(lambda copy: copy.start())

    pl.when(stretch > 0)(wait_for_targets)

    @pl.when((uly == 1) & (to_relay == 0))
    def _():
        each_send(lambda copy: copy.start(), from_hbm)

    for copy in own_copies:
        copy.wait()

    @pl.when((uly == 0) & (stretch > 0))
    def _():
        each_send(lambda copy: copy.start(), from_vmem)

    parts = angle_parts(stretch, rows, span, frequency)
    for copy in gain_copies:
        copy.wait()
    q_gain, k_gain = gains[0] * math.sqrt(head), gains[1] * math.sqrt(head)
    q_swap, k_swap = sign * pltpu.roll(q_gain, half, 1), sign * pltpu.roll(k_gain, half, 1)
    for d in range(span + 1):
        cosine, sine = rope_table(parts, d, rows)
        tab[d + 1, 0], tab[d + 1, 1] = cosine * k_gain, sine * k_swap
        if d == 0:
            tab[0, 0], tab[0, 1] = cosine * q_gain, sine * q_swap

    row = lax.broadcasted_iota(jnp.int32, (rows, rows), 0)
    col = lax.broadcasted_iota(jnp.int32, (rows, rows), 1)
    own = col <= row
    contract = (((1,), (1,)), ((), ()))
    from_lane = lax.broadcasted_iota(jnp.int32, (head, head), 0)
    to_lane = lax.broadcasted_iota(jnp.int32, (head, head), 1)
    swap = (from_lane == lax.rem(to_lane + half, head)).astype(jnp.float32)
    swap = swap.astype(jnp.bfloat16)

    for h in range(kv_heads):
        k_own[h] = rotate(
            kv_own[0, :, h * head : (h + 1) * head], tab[1, 0], tab[1, 1], swap
        )
        values = v_last if h == kv_heads - 1 else v_cat.at[h]
        values[:rows, :head] = kv_own[1, :, h * head : (h + 1) * head]
        values[:, head:] = jnp.ones((values.shape[0], head), jnp.bfloat16)
    for h in range(kv_heads):
        if h == 0:

            @pl.when(stretch == 0)
            def _():
                wait_for_targets()
                each_send(lambda copy: copy.start(), from_vmem)

        if h == kv_heads - 1:
            for late in range(kv_heads):
                pass_on(late, stretch == 2)
        q_copies[h].wait()
        keys = k_own[h]
        for g in range(group):
            if h == 0 and g == 0:

                @pl.when((uly == 1) & (to_relay > 0))
                def _():
                    each_send(lambda copy: copy.start(), from_hbm)

            at = slice(g * rows, (g + 1) * rows)
            q_rot[h, at] = rotate(
                q_buf[h, :, g * head : (g + 1) * head], tab[0, 0], tab[0, 1], swap
            )
            scores = lax.dot_general(
                q_rot[h, at], keys, contract, preferred_element_type=jnp.float32
            )
            tiles[h, 0, at] = jnp.where(own, scores, NEG_FILL)

    scale = math.log2(math.e) / math.sqrt(head)
    keep = col <= row + jnp.where(stretch >= span, 0, rows)
    bias = [
        jnp.where(stretch >= d, 0.0, NEG_FILL).astype(jnp.float32)
        for d in range(1, span)
    ]

    def arrived(h, i):
        for d in range(1, span + 1):
            remote(d, h, i, from_hbm[i]).wait_recv()

    def turn(h):
        for d in range(1, span + 1):
            k_far[h, (d - 1) * rows : d * rows] = rotate(
                kv_prev[d - 1, 0, h], tab[d + 1, 0], tab[d + 1, 1], swap
            )

    def score(h):
        for first in range(0, group, 4):
            at = slice(first * rows, (first + 4) * rows)
            scores = lax.dot_general(
                q_rot[h, at], k_far[h], contract, preferred_element_type=jnp.float32
            )
            tiles[h, 0, at] = jnp.where(
                jnp.concatenate([keep] * 4), tiles[h, 0, at], scores[:, (span - 1) * rows :]
            )
            for d in range(1, span):
                tiles[h, d, at] = scores[:, (d - 1) * rows : d * rows] + bias[d - 1]

    def weigh(h):
        for g in range(group):
            at = slice(g * rows, (g + 1) * rows)
            parts = [tiles[h, d, at] for d in range(span)]
            top = jnp.max(functools.reduce(jnp.maximum, parts), axis=-1, keepdims=True)
            for d in range(span):
                out = w_last if h == kv_heads - 1 else weights.at[h]
                out[d, at] = jnp.exp2((parts[d] - top) * scale).astype(jnp.bfloat16)

    def join(h):
        values = v_last if h == kv_heads - 1 else v_cat.at[h]
        for d in range(1, span + 1):
            values[d * rows : (d + 1) * rows, :head] = kv_prev[d - 1, 1, h]

    def mix(h):
        if h < kv_heads - 1:
            join(h)
            mix_head(weights.at[h], v_cat.at[h], o_ref, h * width, group, None)

    stages = [(0, lambda h: arrived(h, 0)), (0, turn), (1, score), (2, weigh)]
    stages += [(kv_heads, lambda h: arrived(h, 1)), (kv_heads, mix)]
    for step in range(-1, 2 * kv_heads):
        for lag, stage in stages:
            if 0 <= step - lag < kv_heads:
                stage(step - lag)
        for h in range(kv_heads):
            if step == -1:
                pass_on(h, stretch != 2)
    join(kv_heads - 1)

    each_by_relay(lambda copy: copy.wait_send())
    for h in range(kv_heads):

        @pl.when(h >= kv_heads - passed)
        def _(h=h):
            to_target(h).wait_send()

    @pl.when(uly == 1)
    def _():
        each_send(lambda copy: copy.wait_send(), from_hbm)

    @pl.when(uly == 0)
    def _():
        each_send(lambda copy: copy.wait_send(), from_vmem)


def in_hbm(array):
    return pltpu.with_memory_space_constraint(array, pltpu.HBM)


def local(query_proj, key_proj, value_projection, query_gain, key_gain):
    cycle = lax.axis_size("blk")
    span = max(1, cycle // 64)
    rows, head = query_proj.shape[0], query_gain.shape[0]
    kv_heads = key_proj.shape[1] // head
    group = query_proj.shape[1] // head // kv_heads
    bf16, f32 = jnp.bfloat16, jnp.float32
    vmem = pl.BlockSpec(memory_space=pltpu.VMEM)
    hbm = pl.BlockSpec(memory_space=pltpu.HBM)
    most = (kv_heads - 1) * group * head
    o_most, w_last, v_last = pl.pallas_call(
        functools.partial(kernel, cycle, span, kv_heads, group),
        out_shape=[
            jax.ShapeDtypeStruct((rows, most), bf16),
            jax.ShapeDtypeStruct((span, group * rows, rows), bf16),
            jax.ShapeDtypeStruct(((span + 1) * rows, 2 * head), bf16),
        ],
        in_specs=[hbm] * 5,
        out_specs=[vmem] * 3,
        scratch_shapes=[
            pltpu.VMEM((kv_heads, rows, group * head), bf16),
            pltpu.VMEM((2, rows, kv_heads * head), bf16),
            pltpu.VMEM((span, 2, kv_heads, rows, head), bf16),
            pltpu.VMEM((kv_heads, group * rows, head), bf16),
            pltpu.VMEM((kv_heads, rows, head), bf16),
            pltpu.VMEM((kv_heads, span * rows, head), bf16),
            pltpu.VMEM((kv_heads, (span + 1) * rows, 2 * head), bf16),
            pltpu.VMEM((kv_heads, span, group * rows, rows), f32),
            pltpu.VMEM((kv_heads, span, group * rows, rows), bf16),
            pltpu.VMEM((span + 2, 2, rows, head), f32),
            pltpu.VMEM((2, 1, head), f32),
            pltpu.VMEM((kv_heads, rows, head), bf16),
            pltpu.SemaphoreType.DMA((kv_heads,)),
            pltpu.SemaphoreType.DMA((2,)),
            pltpu.SemaphoreType.DMA((2,)),
            pltpu.SemaphoreType.DMA((span, 2, kv_heads)),
            pltpu.SemaphoreType.DMA((span, 2, kv_heads)),
            pltpu.SemaphoreType.DMA((kv_heads,)),
            pltpu.SemaphoreType.DMA((kv_heads,)),
        ],
        compiler_params=pltpu.CompilerParams(
            collective_id=0, has_side_effects=True, vmem_limit_bytes=24 * 1024 * 1024
        ),
        name="window_attention",
    )(
        in_hbm(query_proj),
        in_hbm(key_proj),
        in_hbm(value_projection),
        in_hbm(query_gain.reshape(1, head)),
        in_hbm(key_gain.reshape(1, head)),
    )
    return pl.pallas_call(
        functools.partial(finish, group),
        out_shape=jax.ShapeDtypeStruct(query_proj.shape, bf16),
        in_specs=[vmem] * 3,
        out_specs=hbm,
        scratch_shapes=[
            pltpu.VMEM((rows, group * head), bf16),
            pltpu.SemaphoreType.DMA((3,)),
        ],
        compiler_params=pltpu.CompilerParams(vmem_limit_bytes=8 * 1024 * 1024),
        name="last_heads",
    )(o_most, w_last, v_last)


def solution(mesh):
    rows = P(("groups", "blk", "uly"), None)
    return jax.shard_map(
        local,
        mesh=mesh,
        in_specs=(rows, rows, rows, P(), P()),
        out_specs=rows,
        check_vma=False,
    )
```

```python
import functools
import math

import jax
import jax.numpy as jnp
from jax import lax
from jax.experimental import pallas as pl
from jax.experimental.pallas import tpu as pltpu
from jax.sharding import PartitionSpec as P

NEG_FILL = -1e30
ROPE_BASE = 1000000.0
EPS = 1e-06
MESH = pl.DeviceIdType.MESH


def angle_parts(stretch, rows, span, frequency):
    steps = rows // 8
    count = 8 + steps + 8 * pl.cdiv(span + 1, 8)
    index = lax.broadcasted_iota(jnp.int32, (count, frequency.shape[1]), 0)
    offset = jnp.where(
        index < 8,
        index,
        jnp.where(index < 8 + steps, (index - 8) * 8, (stretch - (index - 8 - steps)) * rows),
    )
    angle = offset.astype(jnp.float32) * frequency
    return jnp.cos(angle), jnp.sin(angle)


def rope_table(parts, d, rows):
    cosine, sine = parts
    steps = rows // 8
    fine_cos, fine_sin = cosine[:8], sine[:8]
    eights_cos, eights_sin = cosine[8 : 8 + steps], sine[8 : 8 + steps]
    at = 8 + steps + d
    first_cos, first_sin = cosine[at : at + 1], sine[at : at + 1]
    coarse_cos = eights_cos * first_cos - eights_sin * first_sin
    coarse_sin = eights_sin * first_cos + eights_cos * first_sin
    cosines, sines = [], []
    for j in range(steps):
        cos_j, sin_j = coarse_cos[j : j + 1], coarse_sin[j : j + 1]
        cosines.append(cos_j * fine_cos - sin_j * fine_sin)
        sines.append(sin_j * fine_cos + cos_j * fine_sin)
    return jnp.concatenate(cosines), jnp.concatenate(sines)


def rotate(x, table_a, table_b, swap):
    swapped = jnp.dot(x, swap, preferred_element_type=jnp.float32)
    x = x.astype(jnp.float32)
    r = lax.rsqrt(jnp.sum(x * x, axis=-1, keepdims=True) + x.shape[1] * EPS)
    return ((x * table_a + swapped * table_b) * r).astype(jnp.bfloat16)


def mix_head(weights, v_cat, o_ref, column, group, ready):
    span, rows, head = weights.shape[0], weights.shape[2], v_cat.shape[1] // 2
    row = lax.broadcasted_iota(jnp.int32, (rows, rows), 0)
    col = lax.broadcasted_iota(jnp.int32, (rows, rows), 1)
    own_mask = (col <= row).astype(jnp.float32).astype(jnp.bfloat16)
    far_mask = 1.0 - own_mask
    values = v_cat[...]
    half = max(1, group // 2)
    for part in range(group // half):
        block = slice(part * half * rows, (part + 1) * half * rows)
        merged = weights[0, block]
        spread = [merged * jnp.concatenate([own_mask] * half)]
        spread += [weights[d, block] for d in range(1, span)]
        spread += [merged * jnp.concatenate([far_mask] * half)]
        mixed = jnp.dot(
            jnp.concatenate(spread, axis=1), values, preferred_element_type=jnp.float32
        )
        for g in range(half):
            piece = mixed[g * rows : (g + 1) * rows]
            at = column + (part * half + g) * head
            o_ref[:, at : at + head] = (piece[:, :head] / piece[:, head:]).astype(
                o_ref.dtype
            )
        if ready is not None:
            ready(part)


def finish(group, o_most, w_last, v_last, o_hbm, o_last, sem):
    width, most = o_last.shape[1], o_most.shape[1]
    copies = [pltpu.make_async_copy(o_most, o_hbm.at[:, pl.ds(0, most)], sem.at[0])]
    copies[0].start()
    half = width // 2

    def ready(part):
        copy = pltpu.make_async_copy(
            o_last.at[:, pl.ds(part * half, half)],
            o_hbm.at[:, pl.ds(most + part * half, half)],
            sem.at[1 + part],
        )
        copy.start()
        copies.append(copy)

    mix_head(w_last, v_last, o_last, 0, group, ready)
    for copy in copies:
        copy.wait()


def kernel(
    cycle, span, kv_heads, group,
    q_hbm, k_hbm, v_hbm, qg_hbm, kg_hbm, o_ref, w_last, v_last,
    q_buf, kv_own, kv_prev, q_rot, k_own, k_far, v_cat, tiles, weights, tab, gains,
    relay_buf, q_sem, own_sem, gain_sem, send_sem, recv_sem, pass_sem, relay_sem,
):
    rows, head = k_hbm.shape[0], qg_hbm.shape[1]
    width = group * head
    blk, uly = lax.axis_index("blk"), lax.axis_index("uly")
    last = 2 * cycle - 1
    stretch = jnp.where(uly == 0, blk, last - blk)
    first_group = lax.axis_index("groups") == 0
    ahead = first_group & (stretch == 0)

    def device_of(index):
        low = index < cycle
        return {"blk": jnp.where(low, index, last - index), "uly": jnp.where(low, 0, 1)}

    barrier = pltpu.get_barrier_semaphore()

    def greet(index):
        pl.semaphore_signal(
            barrier, inc=1, device_id=device_of(index), device_id_type=MESH
        )

    for d in range(1, span + 1):
        pl.when(stretch >= d)(functools.partial(greet, stretch - d))

    def count_between(relay):
        high = (relay >= cycle) & (relay + 2 <= last) & (lax.rem(relay, 2) == 0)
        return jnp.where(high, kv_heads - 1, jnp.where(first_group & (relay == 2), kv_heads - 1, 0))

    relay = jnp.where(stretch == 0, 2, jnp.maximum(stretch - 1, 0))
    odd = (lax.rem(stretch, 2) == 1) & (stretch > cycle)
    to_relay = jnp.where(odd | (stretch == 0), count_between(relay), 0)
    passed = count_between(stretch)
    source = jnp.where(stretch == 2, 0, jnp.minimum(stretch + 1, last))
    target = jnp.where(stretch == 2, 1, jnp.minimum(stretch + 2, last))
    passer = jnp.where(stretch == 1, 2, jnp.maximum(stretch - 2, 0))
    fed = (stretch == 1) | ((lax.rem(stretch, 2) == 0) & (stretch > cycle + 1))
    from_relay = jnp.where(fed, count_between(passer), 0)

    pl.when(from_relay > 0)(functools.partial(greet, passer))
    pl.when(passed > 0)(functools.partial(greet, source))

    own_copies = [
        pltpu.make_async_copy(src, kv_own.at[i], own_sem.at[i])
        for i, src in enumerate((k_hbm, v_hbm))
    ]
    q_copies = [
        pltpu.make_async_copy(
            q_hbm.at[:, pl.ds(h * width, width)], q_buf.at[h], q_sem.at[h]
        )
        for h in range(kv_heads)
    ]
    gain_copies = [
        pltpu.make_async_copy(src, gains.at[i], gain_sem.at[i])
        for i, src in enumerate((qg_hbm, kg_hbm))
    ]

    def remote(d, h, i, src):
        return pltpu.make_async_remote_copy(
            src_ref=src.at[:, pl.ds(h * head, head)],
            dst_ref=kv_prev.at[d - 1, i, h],
            send_sem=send_sem.at[d - 1, i, h],
            recv_sem=recv_sem.at[d - 1, i, h],
            device_id=device_of(stretch + d),
            device_id_type=MESH,
        )

    from_hbm = (k_hbm, v_hbm)
    from_vmem = (kv_own.at[0], kv_own.at[1])

    def each_send(act, sources):
        for i in range(2):
            for h in range(kv_heads):
                for d in range(1, span + 1):
                    sent = stretch + d <= last
                    if d == 1 and i == 1:
                        sent = sent & (h < kv_heads - to_relay)

                    @pl.when(sent)
                    def _(d=d, h=h, i=i):
                        act(remote(d, h, i, sources[i]))

    def to_target(h):
        return pltpu.make_async_remote_copy(
            src_ref=relay_buf.at[h],
            dst_ref=kv_prev.at[0, 1, h],
            send_sem=pass_sem.at[h],
            recv_sem=recv_sem.at[0, 1, h],
            device_id=device_of(target),
            device_id_type=MESH,
        )

    def by_relay(h):
        return pltpu.make_async_remote_copy(
            src_ref=v_hbm.at[:, pl.ds(h * head, head)],
            dst_ref=relay_buf.at[h],
            send_sem=send_sem.at[0, 1, h],
            recv_sem=relay_sem.at[h],
            device_id=device_of(relay),
            device_id_type=MESH,
        )

    def each_by_relay(act):
        for h in range(kv_heads):

            @pl.when(h >= kv_heads - to_relay)
            def _(h=h):
                act(by_relay(h))

    def pass_on(h, when):
        @pl.when(when & (h >= kv_heads - passed))
        def _():
            by_relay(h).wait_recv()
            to_target(h).start()

    for copy in own_copies + gain_copies + q_copies:
        copy.start()

    for d in range(1, span + 1):

        @pl.when(stretch < d)
        def _(d=d):
            for i in range(2):
                for h in range(kv_heads):
                    pltpu.make_async_copy(
                        from_hbm[i].at[:, pl.ds(h * head, head)],
                        kv_prev.at[d - 1, i, h],
                        recv_sem.at[d - 1, i, h],
                    ).start()

    half = head // 2
    lane = lax.broadcasted_iota(jnp.int32, (1, head), 1)
    frequency = jnp.exp(
        lax.rem(lane, half).astype(jnp.float32) * (-2.0 * math.log(ROPE_BASE) / head)
    )
    sign = jnp.where(lane < half, -1.0, 1.0)

    targets = jnp.minimum(span, last - stretch)
    targets += (to_relay > 0).astype(jnp.int32) + (passed > 0).astype(jnp.int32)

    def wait_for_targets():
        @pl.when(targets > 0)
        def _():
            pl.semaphore_wait(barrier, targets)

        each_by_relay(lambda copy: copy.start())

    pl.when(jnp.logical_not(ahead))(wait_for_targets)

    @pl.when((uly == 1) & (to_relay == 0))
    def _():
        each_send(lambda copy: copy.start(), from_hbm)

    for copy in own_copies:
        copy.wait()

    @pl.when((uly == 0) & jnp.logical_not(ahead))
    def _():
        each_send(lambda copy: copy.start(), from_vmem)

    parts = angle_parts(stretch, rows, span, frequency)
    for copy in gain_copies:
        copy.wait()
    q_gain, k_gain = gains[0] * math.sqrt(head), gains[1] * math.sqrt(head)
    q_swap, k_swap = sign * pltpu.roll(q_gain, half, 1), sign * pltpu.roll(k_gain, half, 1)
    for d in range(span + 1):
        cosine, sine = rope_table(parts, d, rows)
        tab[d + 1, 0], tab[d + 1, 1] = cosine * k_gain, sine * k_swap
        if d == 0:
            tab[0, 0], tab[0, 1] = cosine * q_gain, sine * q_swap

    row = lax.broadcasted_iota(jnp.int32, (rows, rows), 0)
    col = lax.broadcasted_iota(jnp.int32, (rows, rows), 1)
    own = col <= row
    contract = (((1,), (1,)), ((), ()))
    from_lane = lax.broadcasted_iota(jnp.int32, (head, head), 0)
    to_lane = lax.broadcasted_iota(jnp.int32, (head, head), 1)
    swap = (from_lane == lax.rem(to_lane + half, head)).astype(jnp.float32)
    swap = swap.astype(jnp.bfloat16)

    for h in range(kv_heads):
        k_own[h] = rotate(
            kv_own[0, :, h * head : (h + 1) * head], tab[1, 0], tab[1, 1], swap
        )
        values = v_last if h == kv_heads - 1 else v_cat.at[h]
        values[:rows, :head] = kv_own[1, :, h * head : (h + 1) * head]
        values[:, head:] = jnp.ones((values.shape[0], head), jnp.bfloat16)
    for h in range(kv_heads):
        if h == 0:

            @pl.when(ahead)
            def _():
                wait_for_targets()
                each_send(lambda copy: copy.start(), from_vmem)

        if h == kv_heads - 1:
            for late in range(kv_heads):
                pass_on(late, stretch == 2)
        q_copies[h].wait()
        keys = k_own[h]
        for g in range(group):
            if h == 0 and g == 0:

                @pl.when((uly == 1) & (to_relay > 0))
                def _():
                    each_send(lambda copy: copy.start(), from_hbm)

            at = slice(g * rows, (g + 1) * rows)
            q_rot[h, at] = rotate(
                q_buf[h, :, g * head : (g + 1) * head], tab[0, 0], tab[0, 1], swap
            )
            scores = lax.dot_general(
                q_rot[h, at], keys, contract, preferred_element_type=jnp.float32
            )
            tiles[h, 0, at] = jnp.where(own, scores, NEG_FILL)

    scale = math.log2(math.e) / math.sqrt(head)
    keep = col <= row + jnp.where(stretch >= span, 0, rows)
    bias = [
        jnp.where(stretch >= d, 0.0, NEG_FILL).astype(jnp.float32)
        for d in range(1, span)
    ]

    def arrived(h, i):
        for d in range(1, span + 1):
            remote(d, h, i, from_hbm[i]).wait_recv()

    def turn(h):
        for d in range(1, span + 1):
            k_far[h, (d - 1) * rows : d * rows] = rotate(
                kv_prev[d - 1, 0, h], tab[d + 1, 0], tab[d + 1, 1], swap
            )

    def score(h):
        for first in range(0, group, 4):
            at = slice(first * rows, (first + 4) * rows)
            scores = lax.dot_general(
                q_rot[h, at], k_far[h], contract, preferred_element_type=jnp.float32
            )
            tiles[h, 0, at] = jnp.where(
                jnp.concatenate([keep] * 4), tiles[h, 0, at], scores[:, (span - 1) * rows :]
            )
            for d in range(1, span):
                tiles[h, d, at] = scores[:, (d - 1) * rows : d * rows] + bias[d - 1]

    def weigh(h):
        for g in range(group):
            at = slice(g * rows, (g + 1) * rows)
            parts = [tiles[h, d, at] for d in range(span)]
            top = jnp.max(functools.reduce(jnp.maximum, parts), axis=-1, keepdims=True)
            for d in range(span):
                out = w_last if h == kv_heads - 1 else weights.at[h]
                out[d, at] = jnp.exp2((parts[d] - top) * scale).astype(jnp.bfloat16)

    def join(h):
        values = v_last if h == kv_heads - 1 else v_cat.at[h]
        for d in range(1, span + 1):
            values[d * rows : (d + 1) * rows, :head] = kv_prev[d - 1, 1, h]

    def mix(h):
        if h < kv_heads - 1:
            join(h)
            mix_head(weights.at[h], v_cat.at[h], o_ref, h * width, group, None)

    stages = [(0, lambda h: arrived(h, 0)), (0, turn), (1, score), (2, weigh)]
    stages += [(kv_heads, lambda h: arrived(h, 1)), (kv_heads, mix)]
    for step in range(-1, 2 * kv_heads):
        for lag, stage in stages:
            if 0 <= step - lag < kv_heads:
                stage(step - lag)
        for h in range(kv_heads):
            if step == -1:
                pass_on(h, stretch != 2)
    join(kv_heads - 1)

    each_by_relay(lambda copy: copy.wait_send())
    for h in range(kv_heads):

        @pl.when(h >= kv_heads - passed)
        def _(h=h):
            to_target(h).wait_send()

    @pl.when(uly == 1)
    def _():
        each_send(lambda copy: copy.wait_send(), from_hbm)

    @pl.when(uly == 0)
    def _():
        each_send(lambda copy: copy.wait_send(), from_vmem)


def in_hbm(array):
    return pltpu.with_memory_space_constraint(array, pltpu.HBM)


def local(query_proj, key_proj, value_projection, query_gain, key_gain):
    cycle = lax.axis_size("blk")
    span = max(1, cycle // 64)
    rows, head = query_proj.shape[0], query_gain.shape[0]
    kv_heads = key_proj.shape[1] // head
    group = query_proj.shape[1] // head // kv_heads
    bf16, f32 = jnp.bfloat16, jnp.float32
    vmem = pl.BlockSpec(memory_space=pltpu.VMEM)
    hbm = pl.BlockSpec(memory_space=pltpu.HBM)
    most = (kv_heads - 1) * group * head
    o_most, w_last, v_last = pl.pallas_call(
        functools.partial(kernel, cycle, span, kv_heads, group),
        out_shape=[
            jax.ShapeDtypeStruct((rows, most), bf16),
            jax.ShapeDtypeStruct((span, group * rows, rows), bf16),
            jax.ShapeDtypeStruct(((span + 1) * rows, 2 * head), bf16),
        ],
        in_specs=[hbm] * 5,
        out_specs=[vmem] * 3,
        scratch_shapes=[
            pltpu.VMEM((kv_heads, rows, group * head), bf16),
            pltpu.VMEM((2, rows, kv_heads * head), bf16),
            pltpu.VMEM((span, 2, kv_heads, rows, head), bf16),
            pltpu.VMEM((kv_heads, group * rows, head), bf16),
            pltpu.VMEM((kv_heads, rows, head), bf16),
            pltpu.VMEM((kv_heads, span * rows, head), bf16),
            pltpu.VMEM((kv_heads, (span + 1) * rows, 2 * head), bf16),
            pltpu.VMEM((kv_heads, span, group * rows, rows), f32),
            pltpu.VMEM((kv_heads, span, group * rows, rows), bf16),
            pltpu.VMEM((span + 2, 2, rows, head), f32),
            pltpu.VMEM((2, 1, head), f32),
            pltpu.VMEM((kv_heads, rows, head), bf16),
            pltpu.SemaphoreType.DMA((kv_heads,)),
            pltpu.SemaphoreType.DMA((2,)),
            pltpu.SemaphoreType.DMA((2,)),
            pltpu.SemaphoreType.DMA((span, 2, kv_heads)),
            pltpu.SemaphoreType.DMA((span, 2, kv_heads)),
            pltpu.SemaphoreType.DMA((kv_heads,)),
            pltpu.SemaphoreType.DMA((kv_heads,)),
        ],
        compiler_params=pltpu.CompilerParams(
            collective_id=0, has_side_effects=True, vmem_limit_bytes=24 * 1024 * 1024
        ),
        name="window_attention",
    )(
        in_hbm(query_proj),
        in_hbm(key_proj),
        in_hbm(value_projection),
        in_hbm(query_gain.reshape(1, head)),
        in_hbm(key_gain.reshape(1, head)),
    )
    return pl.pallas_call(
        functools.partial(finish, group),
        out_shape=jax.ShapeDtypeStruct(query_proj.shape, bf16),
        in_specs=[vmem] * 3,
        out_specs=hbm,
        scratch_shapes=[
            pltpu.VMEM((rows, group * head), bf16),
            pltpu.SemaphoreType.DMA((3,)),
        ],
        compiler_params=pltpu.CompilerParams(vmem_limit_bytes=8 * 1024 * 1024),
        name="last_heads",
    )(o_most, w_last, v_last)


def solution(mesh):
    rows = P(("groups", "blk", "uly"), None)
    return jax.shard_map(
        local,
        mesh=mesh,
        in_specs=(rows, rows, rows, P(), P()),
        out_specs=rows,
        check_vma=False,
    )
```

```python
import functools
import math

import jax
import jax.numpy as jnp
from jax import lax
from jax.experimental import pallas as pl
from jax.experimental.pallas import tpu as pltpu
from jax.sharding import PartitionSpec as P

NEG_FILL = -1e30
ROPE_BASE = 1000000.0
EPS = 1e-06
MESH = pl.DeviceIdType.MESH


def angle_parts(stretch, rows, span, frequency):
    steps = rows // 8
    count = 8 + steps + 8 * pl.cdiv(span + 1, 8)
    index = lax.broadcasted_iota(jnp.int32, (count, frequency.shape[1]), 0)
    offset = jnp.where(
        index < 8,
        index,
        jnp.where(index < 8 + steps, (index - 8) * 8, (stretch - (index - 8 - steps)) * rows),
    )
    angle = offset.astype(jnp.float32) * frequency
    return jnp.cos(angle), jnp.sin(angle)


def rope_table(parts, d, rows):
    cosine, sine = parts
    steps = rows // 8
    fine_cos, fine_sin = cosine[:8], sine[:8]
    eights_cos, eights_sin = cosine[8 : 8 + steps], sine[8 : 8 + steps]
    at = 8 + steps + d
    first_cos, first_sin = cosine[at : at + 1], sine[at : at + 1]
    coarse_cos = eights_cos * first_cos - eights_sin * first_sin
    coarse_sin = eights_sin * first_cos + eights_cos * first_sin
    cosines, sines = [], []
    for j in range(steps):
        cos_j, sin_j = coarse_cos[j : j + 1], coarse_sin[j : j + 1]
        cosines.append(cos_j * fine_cos - sin_j * fine_sin)
        sines.append(sin_j * fine_cos + cos_j * fine_sin)
    return jnp.concatenate(cosines), jnp.concatenate(sines)


def rotate(x, table_a, table_b, swap):
    swapped = jnp.dot(x, swap, preferred_element_type=jnp.float32)
    x = x.astype(jnp.float32)
    r = lax.rsqrt(jnp.sum(x * x, axis=-1, keepdims=True) + x.shape[1] * EPS)
    return ((x * table_a + swapped * table_b) * r).astype(jnp.bfloat16)


def mix_head(weights, v_cat, o_ref, column, group, ready):
    span, rows, head = weights.shape[0], weights.shape[2], v_cat.shape[1] // 2
    row = lax.broadcasted_iota(jnp.int32, (rows, rows), 0)
    col = lax.broadcasted_iota(jnp.int32, (rows, rows), 1)
    own_mask = (col <= row).astype(jnp.float32).astype(jnp.bfloat16)
    far_mask = 1.0 - own_mask
    values = v_cat[...]
    heads = max(1, group // (2 if ready is None else 4))
    for part in range(group // heads):
        block = slice(part * heads * rows, (part + 1) * heads * rows)
        merged = weights[0, block]
        spread = [merged * jnp.concatenate([own_mask] * heads)]
        spread += [weights[d, block] for d in range(1, span)]
        spread += [merged * jnp.concatenate([far_mask] * heads)]
        mixed = jnp.dot(
            jnp.concatenate(spread, axis=1), values, preferred_element_type=jnp.float32
        )
        for g in range(heads):
            piece = mixed[g * rows : (g + 1) * rows]
            at = column + (part * heads + g) * head
            o_ref[:, at : at + head] = (piece[:, :head] / piece[:, head:]).astype(
                o_ref.dtype
            )
        if ready is not None:
            ready(part)


def finish(group, o_most, w_last, v_last, o_hbm, o_last, sem):
    width, most = o_last.shape[1], o_most.shape[1]
    copies = [pltpu.make_async_copy(o_most, o_hbm.at[:, pl.ds(0, most)], sem.at[0])]
    copies[0].start()
    quarter = width // 4

    def ready(part):
        copy = pltpu.make_async_copy(
            o_last.at[:, pl.ds(part * quarter, quarter)],
            o_hbm.at[:, pl.ds(most + part * quarter, quarter)],
            sem.at[1 + part],
        )
        copy.start()
        copies.append(copy)

    mix_head(w_last, v_last, o_last, 0, group, ready)
    for copy in copies:
        copy.wait()


def kernel(
    cycle, span, kv_heads, group,
    q_hbm, k_hbm, v_hbm, qg_hbm, kg_hbm, o_ref, w_last, v_last,
    q_buf, kv_own, kv_prev, q_rot, k_own, k_far, v_cat, tiles, weights, tab, gains,
    relay_buf, q_sem, own_sem, gain_sem, send_sem, recv_sem, pass_sem, relay_sem,
):
    rows, head = k_hbm.shape[0], qg_hbm.shape[1]
    width = group * head
    blk, uly = lax.axis_index("blk"), lax.axis_index("uly")
    last = 2 * cycle - 1
    stretch = jnp.where(uly == 0, blk, last - blk)
    first_group = lax.axis_index("groups") == 0
    ahead = first_group & (stretch == 0)

    def device_of(index):
        low = index < cycle
        return {"blk": jnp.where(low, index, last - index), "uly": jnp.where(low, 0, 1)}

    barrier = pltpu.get_barrier_semaphore()

    def greet(index):
        pl.semaphore_signal(
            barrier, inc=1, device_id=device_of(index), device_id_type=MESH
        )

    for d in range(1, span + 1):
        pl.when(stretch >= d)(functools.partial(greet, stretch - d))

    def count_between(relay):
        high = (relay >= cycle) & (relay + 2 <= last) & (lax.rem(relay, 2) == 0)
        return jnp.where(high, kv_heads - 1, jnp.where(first_group & (relay == 2), kv_heads - 1, 0))

    relay = jnp.where(stretch == 0, 2, jnp.maximum(stretch - 1, 0))
    odd = (lax.rem(stretch, 2) == 1) & (stretch > cycle)
    to_relay = jnp.where(odd | (stretch == 0), count_between(relay), 0)
    passed = count_between(stretch)
    source = jnp.where(stretch == 2, 0, jnp.minimum(stretch + 1, last))
    target = jnp.where(stretch == 2, 1, jnp.minimum(stretch + 2, last))
    passer = jnp.where(stretch == 1, 2, jnp.maximum(stretch - 2, 0))
    fed = (stretch == 1) | ((lax.rem(stretch, 2) == 0) & (stretch > cycle + 1))
    from_relay = jnp.where(fed, count_between(passer), 0)

    pl.when(from_relay > 0)(functools.partial(greet, passer))
    pl.when(passed > 0)(functools.partial(greet, source))

    own_copies = [
        pltpu.make_async_copy(src, kv_own.at[i], own_sem.at[i])
        for i, src in enumerate((k_hbm, v_hbm))
    ]
    q_copies = [
        pltpu.make_async_copy(
            q_hbm.at[:, pl.ds(h * width, width)], q_buf.at[h], q_sem.at[h]
        )
        for h in range(kv_heads)
    ]
    gain_copies = [
        pltpu.make_async_copy(src, gains.at[i], gain_sem.at[i])
        for i, src in enumerate((qg_hbm, kg_hbm))
    ]

    def remote(d, h, i, src):
        return pltpu.make_async_remote_copy(
            src_ref=src.at[:, pl.ds(h * head, head)],
            dst_ref=kv_prev.at[d - 1, i, h],
            send_sem=send_sem.at[d - 1, i, h],
            recv_sem=recv_sem.at[d - 1, i, h],
            device_id=device_of(stretch + d),
            device_id_type=MESH,
        )

    from_hbm = (k_hbm, v_hbm)
    from_vmem = (kv_own.at[0], kv_own.at[1])

    def each_send(act, sources):
        for i in range(2):
            for h in range(kv_heads):
                for d in range(1, span + 1):
                    sent = stretch + d <= last
                    if d == 1 and i == 1:
                        sent = sent & (h < kv_heads - to_relay)

                    @pl.when(sent)
                    def _(d=d, h=h, i=i):
                        act(remote(d, h, i, sources[i]))

    def to_target(h):
        return pltpu.make_async_remote_copy(
            src_ref=relay_buf.at[h],
            dst_ref=kv_prev.at[0, 1, h],
            send_sem=pass_sem.at[h],
            recv_sem=recv_sem.at[0, 1, h],
            device_id=device_of(target),
            device_id_type=MESH,
        )

    def by_relay(h):
        return pltpu.make_async_remote_copy(
            src_ref=v_hbm.at[:, pl.ds(h * head, head)],
            dst_ref=relay_buf.at[h],
            send_sem=send_sem.at[0, 1, h],
            recv_sem=relay_sem.at[h],
            device_id=device_of(relay),
            device_id_type=MESH,
        )

    def each_by_relay(act):
        for h in range(kv_heads):

            @pl.when(h >= kv_heads - to_relay)
            def _(h=h):
                act(by_relay(h))

    def pass_on(h, when):
        @pl.when(when & (h >= kv_heads - passed))
        def _():
            by_relay(h).wait_recv()
            to_target(h).start()

    for copy in own_copies + gain_copies + q_copies:
        copy.start()

    for d in range(1, span + 1):

        @pl.when(stretch < d)
        def _(d=d):
            for i in range(2):
                for h in range(kv_heads):
                    pltpu.make_async_copy(
                        from_hbm[i].at[:, pl.ds(h * head, head)],
                        kv_prev.at[d - 1, i, h],
                        recv_sem.at[d - 1, i, h],
                    ).start()

    half = head // 2
    lane = lax.broadcasted_iota(jnp.int32, (1, head), 1)
    frequency = jnp.exp(
        lax.rem(lane, half).astype(jnp.float32) * (-2.0 * math.log(ROPE_BASE) / head)
    )
    sign = jnp.where(lane < half, -1.0, 1.0)

    targets = jnp.minimum(span, last - stretch)
    targets += (to_relay > 0).astype(jnp.int32) + (passed > 0).astype(jnp.int32)

    def wait_for_targets():
        @pl.when(targets > 0)
        def _():
            pl.semaphore_wait(barrier, targets)

        each_by_relay(lambda copy: copy.start())

    pl.when(jnp.logical_not(ahead))(wait_for_targets)

    @pl.when((uly == 1) & (to_relay == 0))
    def _():
        each_send(lambda copy: copy.start(), from_hbm)

    for copy in own_copies:
        copy.wait()

    @pl.when((uly == 0) & jnp.logical_not(ahead))
    def _():
        each_send(lambda copy: copy.start(), from_vmem)

    parts = angle_parts(stretch, rows, span, frequency)
    for copy in gain_copies:
        copy.wait()
    q_gain, k_gain = gains[0] * math.sqrt(head), gains[1] * math.sqrt(head)
    q_swap, k_swap = sign * pltpu.roll(q_gain, half, 1), sign * pltpu.roll(k_gain, half, 1)
    for d in range(span + 1):
        cosine, sine = rope_table(parts, d, rows)
        tab[d + 1, 0], tab[d + 1, 1] = cosine * k_gain, sine * k_swap
        if d == 0:
            tab[0, 0], tab[0, 1] = cosine * q_gain, sine * q_swap

    row = lax.broadcasted_iota(jnp.int32, (rows, rows), 0)
    col = lax.broadcasted_iota(jnp.int32, (rows, rows), 1)
    own = col <= row
    contract = (((1,), (1,)), ((), ()))
    from_lane = lax.broadcasted_iota(jnp.int32, (head, head), 0)
    to_lane = lax.broadcasted_iota(jnp.int32, (head, head), 1)
    swap = (from_lane == lax.rem(to_lane + half, head)).astype(jnp.float32)
    swap = swap.astype(jnp.bfloat16)

    for h in range(kv_heads):
        k_own[h] = rotate(
            kv_own[0, :, h * head : (h + 1) * head], tab[1, 0], tab[1, 1], swap
        )
        values = v_last if h == kv_heads - 1 else v_cat.at[h]
        values[:rows, :head] = kv_own[1, :, h * head : (h + 1) * head]
        values[:, head:] = jnp.ones((values.shape[0], head), jnp.bfloat16)
    for h in range(kv_heads):
        if h == 0:

            @pl.when(ahead)
            def _():
                wait_for_targets()
                each_send(lambda copy: copy.start(), from_vmem)

        if h == kv_heads - 1:
            for late in range(kv_heads):
                pass_on(late, stretch == 2)
        q_copies[h].wait()
        keys = k_own[h]
        for g in range(group):
            if h == 0 and g == 0:

                @pl.when((uly == 1) & (to_relay > 0))
                def _():
                    each_send(lambda copy: copy.start(), from_hbm)

            at = slice(g * rows, (g + 1) * rows)
            q_rot[h, at] = rotate(
                q_buf[h, :, g * head : (g + 1) * head], tab[0, 0], tab[0, 1], swap
            )
            scores = lax.dot_general(
                q_rot[h, at], keys, contract, preferred_element_type=jnp.float32
            )
            tiles[h, 0, at] = jnp.where(own, scores, NEG_FILL)

    scale = math.log2(math.e) / math.sqrt(head)
    keep = col <= row + jnp.where(stretch >= span, 0, rows)
    bias = [
        jnp.where(stretch >= d, 0.0, NEG_FILL).astype(jnp.float32)
        for d in range(1, span)
    ]

    def arrived(h, i):
        for d in range(1, span + 1):
            remote(d, h, i, from_hbm[i]).wait_recv()

    def turn(h):
        for d in range(1, span + 1):
            k_far[h, (d - 1) * rows : d * rows] = rotate(
                kv_prev[d - 1, 0, h], tab[d + 1, 0], tab[d + 1, 1], swap
            )

    def score(h):
        for first in range(0, group, 4):
            at = slice(first * rows, (first + 4) * rows)
            scores = lax.dot_general(
                q_rot[h, at], k_far[h], contract, preferred_element_type=jnp.float32
            )
            tiles[h, 0, at] = jnp.where(
                jnp.concatenate([keep] * 4), tiles[h, 0, at], scores[:, (span - 1) * rows :]
            )
            for d in range(1, span):
                tiles[h, d, at] = scores[:, (d - 1) * rows : d * rows] + bias[d - 1]

    def weigh(h):
        for g in range(group):
            at = slice(g * rows, (g + 1) * rows)
            parts = [tiles[h, d, at] for d in range(span)]
            top = jnp.max(functools.reduce(jnp.maximum, parts), axis=-1, keepdims=True)
            for d in range(span):
                out = w_last if h == kv_heads - 1 else weights.at[h]
                out[d, at] = jnp.exp2((parts[d] - top) * scale).astype(jnp.bfloat16)

    def join(h):
        values = v_last if h == kv_heads - 1 else v_cat.at[h]
        for d in range(1, span + 1):
            values[d * rows : (d + 1) * rows, :head] = kv_prev[d - 1, 1, h]

    def mix(h):
        if h < kv_heads - 1:
            join(h)
            mix_head(weights.at[h], v_cat.at[h], o_ref, h * width, group, None)

    stages = [(0, lambda h: arrived(h, 0)), (0, turn), (1, score), (2, weigh)]
    stages += [(kv_heads, lambda h: arrived(h, 1)), (kv_heads, mix)]
    for step in range(-1, 2 * kv_heads):
        for lag, stage in stages:
            if 0 <= step - lag < kv_heads:
                stage(step - lag)
        for h in range(kv_heads):
            if step == -1:
                pass_on(h, stretch != 2)
    join(kv_heads - 1)

    each_by_relay(lambda copy: copy.wait_send())
    for h in range(kv_heads):

        @pl.when(h >= kv_heads - passed)
        def _(h=h):
            to_target(h).wait_send()

    @pl.when(uly == 1)
    def _():
        each_send(lambda copy: copy.wait_send(), from_hbm)

    @pl.when(uly == 0)
    def _():
        each_send(lambda copy: copy.wait_send(), from_vmem)


def in_hbm(array):
    return pltpu.with_memory_space_constraint(array, pltpu.HBM)


def local(query_proj, key_proj, value_projection, query_gain, key_gain):
    cycle = lax.axis_size("blk")
    span = max(1, cycle // 64)
    rows, head = query_proj.shape[0], query_gain.shape[0]
    kv_heads = key_proj.shape[1] // head
    group = query_proj.shape[1] // head // kv_heads
    bf16, f32 = jnp.bfloat16, jnp.float32
    vmem = pl.BlockSpec(memory_space=pltpu.VMEM)
    hbm = pl.BlockSpec(memory_space=pltpu.HBM)
    most = (kv_heads - 1) * group * head
    o_most, w_last, v_last = pl.pallas_call(
        functools.partial(kernel, cycle, span, kv_heads, group),
        out_shape=[
            jax.ShapeDtypeStruct((rows, most), bf16),
            jax.ShapeDtypeStruct((span, group * rows, rows), bf16),
            jax.ShapeDtypeStruct(((span + 1) * rows, 2 * head), bf16),
        ],
        in_specs=[hbm] * 5,
        out_specs=[vmem] * 3,
        scratch_shapes=[
            pltpu.VMEM((kv_heads, rows, group * head), bf16),
            pltpu.VMEM((2, rows, kv_heads * head), bf16),
            pltpu.VMEM((span, 2, kv_heads, rows, head), bf16),
            pltpu.VMEM((kv_heads, group * rows, head), bf16),
            pltpu.VMEM((kv_heads, rows, head), bf16),
            pltpu.VMEM((kv_heads, span * rows, head), bf16),
            pltpu.VMEM((kv_heads, (span + 1) * rows, 2 * head), bf16),
            pltpu.VMEM((kv_heads, span, group * rows, rows), f32),
            pltpu.VMEM((kv_heads, span, group * rows, rows), bf16),
            pltpu.VMEM((span + 2, 2, rows, head), f32),
            pltpu.VMEM((2, 1, head), f32),
            pltpu.VMEM((kv_heads, rows, head), bf16),
            pltpu.SemaphoreType.DMA((kv_heads,)),
            pltpu.SemaphoreType.DMA((2,)),
            pltpu.SemaphoreType.DMA((2,)),
            pltpu.SemaphoreType.DMA((span, 2, kv_heads)),
            pltpu.SemaphoreType.DMA((span, 2, kv_heads)),
            pltpu.SemaphoreType.DMA((kv_heads,)),
            pltpu.SemaphoreType.DMA((kv_heads,)),
        ],
        compiler_params=pltpu.CompilerParams(
            collective_id=0, has_side_effects=True, vmem_limit_bytes=24 * 1024 * 1024
        ),
        name="window_attention",
    )(
        in_hbm(query_proj),
        in_hbm(key_proj),
        in_hbm(value_projection),
        in_hbm(query_gain.reshape(1, head)),
        in_hbm(key_gain.reshape(1, head)),
    )
    return pl.pallas_call(
        functools.partial(finish, group),
        out_shape=jax.ShapeDtypeStruct(query_proj.shape, bf16),
        in_specs=[vmem] * 3,
        out_specs=hbm,
        scratch_shapes=[
            pltpu.VMEM((rows, group * head), bf16),
            pltpu.SemaphoreType.DMA((5,)),
        ],
        compiler_params=pltpu.CompilerParams(vmem_limit_bytes=8 * 1024 * 1024),
        name="last_heads",
    )(o_most, w_last, v_last)


def solution(mesh):
    rows = P(("groups", "blk", "uly"), None)
    return jax.shard_map(
        local,
        mesh=mesh,
        in_specs=(rows, rows, rows, P(), P()),
        out_specs=rows,
        check_vma=False,
    )
```

```python
import functools
import math

import jax
import jax.numpy as jnp
from jax import lax
from jax.experimental import pallas as pl
from jax.experimental.pallas import tpu as pltpu
from jax.sharding import PartitionSpec as P

NEG_FILL = -1e30
ROPE_BASE = 1000000.0
EPS = 1e-06
MESH = pl.DeviceIdType.MESH


def angle_parts(stretch, rows, span, frequency):
    steps = rows // 8
    count = 8 + steps + 8 * pl.cdiv(span + 1, 8)
    index = lax.broadcasted_iota(jnp.int32, (count, frequency.shape[1]), 0)
    offset = jnp.where(
        index < 8,
        index,
        jnp.where(index < 8 + steps, (index - 8) * 8, (stretch - (index - 8 - steps)) * rows),
    )
    angle = offset.astype(jnp.float32) * frequency
    return jnp.cos(angle), jnp.sin(angle)


def rope_table(parts, d, rows):
    cosine, sine = parts
    steps = rows // 8
    fine_cos, fine_sin = cosine[:8], sine[:8]
    eights_cos, eights_sin = cosine[8 : 8 + steps], sine[8 : 8 + steps]
    at = 8 + steps + d
    first_cos, first_sin = cosine[at : at + 1], sine[at : at + 1]
    coarse_cos = eights_cos * first_cos - eights_sin * first_sin
    coarse_sin = eights_sin * first_cos + eights_cos * first_sin
    cosines, sines = [], []
    for j in range(steps):
        cos_j, sin_j = coarse_cos[j : j + 1], coarse_sin[j : j + 1]
        cosines.append(cos_j * fine_cos - sin_j * fine_sin)
        sines.append(sin_j * fine_cos + cos_j * fine_sin)
    return jnp.concatenate(cosines), jnp.concatenate(sines)


def rotate(x, table_a, table_b, swap):
    swapped = jnp.dot(x, swap, preferred_element_type=jnp.float32)
    x = x.astype(jnp.float32)
    r = lax.rsqrt(jnp.sum(x * x, axis=-1, keepdims=True) + x.shape[1] * EPS)
    return ((x * table_a + swapped * table_b) * r).astype(jnp.bfloat16)


def mix_head(weights, v_cat, o_ref, column, group, ready):
    span, rows, head = weights.shape[0], weights.shape[2], v_cat.shape[1] // 2
    row = lax.broadcasted_iota(jnp.int32, (rows, rows), 0)
    col = lax.broadcasted_iota(jnp.int32, (rows, rows), 1)
    own_mask = (col <= row).astype(jnp.float32).astype(jnp.bfloat16)
    far_mask = 1.0 - own_mask
    values = v_cat[...]
    heads = max(1, group // 4)
    for part in range(group // heads):
        block = slice(part * heads * rows, (part + 1) * heads * rows)
        merged = weights[0, block]
        spread = [merged * jnp.concatenate([own_mask] * heads)]
        spread += [weights[d, block] for d in range(1, span)]
        spread += [merged * jnp.concatenate([far_mask] * heads)]
        mixed = jnp.dot(
            jnp.concatenate(spread, axis=1), values, preferred_element_type=jnp.float32
        )
        for g in range(heads):
            piece = mixed[g * rows : (g + 1) * rows]
            at = column + (part * heads + g) * head
            o_ref[:, at : at + head] = (piece[:, :head] / piece[:, head:]).astype(
                o_ref.dtype
            )
        if ready is not None:
            ready(part)


def finish(group, o_most, w_last, v_last, o_hbm, o_last, sem):
    width, most = o_last.shape[1], o_most.shape[1]
    copies = [pltpu.make_async_copy(o_most, o_hbm.at[:, pl.ds(0, most)], sem.at[0])]
    copies[0].start()
    quarter = width // 4

    def ready(part):
        copy = pltpu.make_async_copy(
            o_last.at[:, pl.ds(part * quarter, quarter)],
            o_hbm.at[:, pl.ds(most + part * quarter, quarter)],
            sem.at[1 + part],
        )
        copy.start()
        copies.append(copy)

    mix_head(w_last, v_last, o_last, 0, group, ready)
    for copy in copies:
        copy.wait()


def kernel(
    cycle, span, kv_heads, group,
    q_hbm, k_hbm, v_hbm, qg_hbm, kg_hbm, o_ref, w_last, v_last,
    q_buf, kv_own, kv_prev, q_rot, k_own, k_far, v_cat, tiles, weights, tab, gains,
    relay_buf, q_sem, own_sem, gain_sem, send_sem, recv_sem, pass_sem, relay_sem,
):
    rows, head = k_hbm.shape[0], qg_hbm.shape[1]
    width = group * head
    blk, uly = lax.axis_index("blk"), lax.axis_index("uly")
    last = 2 * cycle - 1
    stretch = jnp.where(uly == 0, blk, last - blk)
    first_group = lax.axis_index("groups") == 0
    ahead = first_group & (stretch == 0)

    def device_of(index):
        low = index < cycle
        return {"blk": jnp.where(low, index, last - index), "uly": jnp.where(low, 0, 1)}

    barrier = pltpu.get_barrier_semaphore()

    def greet(index):
        pl.semaphore_signal(
            barrier, inc=1, device_id=device_of(index), device_id_type=MESH
        )

    for d in range(1, span + 1):
        pl.when(stretch >= d)(functools.partial(greet, stretch - d))

    def count_between(relay):
        high = (relay >= cycle) & (relay + 2 <= last) & (lax.rem(relay, 2) == 0)
        return jnp.where(high, kv_heads - 1, jnp.where(first_group & (relay == 2), kv_heads - 1, 0))

    relay = jnp.where(stretch == 0, 2, jnp.maximum(stretch - 1, 0))
    odd = (lax.rem(stretch, 2) == 1) & (stretch > cycle)
    to_relay = jnp.where(odd | (stretch == 0), count_between(relay), 0)
    passed = count_between(stretch)
    source = jnp.where(stretch == 2, 0, jnp.minimum(stretch + 1, last))
    target = jnp.where(stretch == 2, 1, jnp.minimum(stretch + 2, last))
    passer = jnp.where(stretch == 1, 2, jnp.maximum(stretch - 2, 0))
    fed = (stretch == 1) | ((lax.rem(stretch, 2) == 0) & (stretch > cycle + 1))
    from_relay = jnp.where(fed, count_between(passer), 0)

    pl.when(from_relay > 0)(functools.partial(greet, passer))
    pl.when(passed > 0)(functools.partial(greet, source))

    own_copies = [
        pltpu.make_async_copy(src, kv_own.at[i], own_sem.at[i])
        for i, src in enumerate((k_hbm, v_hbm))
    ]
    q_copies = [
        pltpu.make_async_copy(
            q_hbm.at[:, pl.ds(h * width, width)], q_buf.at[h], q_sem.at[h]
        )
        for h in range(kv_heads)
    ]
    gain_copies = [
        pltpu.make_async_copy(src, gains.at[i], gain_sem.at[i])
        for i, src in enumerate((qg_hbm, kg_hbm))
    ]

    def remote(d, h, i, src):
        return pltpu.make_async_remote_copy(
            src_ref=src.at[:, pl.ds(h * head, head)],
            dst_ref=kv_prev.at[d - 1, i, h],
            send_sem=send_sem.at[d - 1, i, h],
            recv_sem=recv_sem.at[d - 1, i, h],
            device_id=device_of(stretch + d),
            device_id_type=MESH,
        )

    from_hbm = (k_hbm, v_hbm)
    from_vmem = (kv_own.at[0], kv_own.at[1])

    def each_send(act, sources):
        for i in range(2):
            for h in range(kv_heads):
                for d in range(1, span + 1):
                    sent = stretch + d <= last
                    if d == 1 and i == 1:
                        sent = sent & (h < kv_heads - to_relay)

                    @pl.when(sent)
                    def _(d=d, h=h, i=i):
                        act(remote(d, h, i, sources[i]))

    def to_target(h):
        return pltpu.make_async_remote_copy(
            src_ref=relay_buf.at[h],
            dst_ref=kv_prev.at[0, 1, h],
            send_sem=pass_sem.at[h],
            recv_sem=recv_sem.at[0, 1, h],
            device_id=device_of(target),
            device_id_type=MESH,
        )

    def by_relay(h):
        return pltpu.make_async_remote_copy(
            src_ref=v_hbm.at[:, pl.ds(h * head, head)],
            dst_ref=relay_buf.at[h],
            send_sem=send_sem.at[0, 1, h],
            recv_sem=relay_sem.at[h],
            device_id=device_of(relay),
            device_id_type=MESH,
        )

    def each_by_relay(act):
        for h in range(kv_heads):

            @pl.when(h >= kv_heads - to_relay)
            def _(h=h):
                act(by_relay(h))

    def pass_on(h, when):
        @pl.when(when & (h >= kv_heads - passed))
        def _():
            by_relay(h).wait_recv()
            to_target(h).start()

    for copy in own_copies + gain_copies + q_copies:
        copy.start()

    for d in range(1, span + 1):

        @pl.when(stretch < d)
        def _(d=d):
            for i in range(2):
                for h in range(kv_heads):
                    pltpu.make_async_copy(
                        from_hbm[i].at[:, pl.ds(h * head, head)],
                        kv_prev.at[d - 1, i, h],
                        recv_sem.at[d - 1, i, h],
                    ).start()

    half = head // 2
    lane = lax.broadcasted_iota(jnp.int32, (1, head), 1)
    frequency = jnp.exp(
        lax.rem(lane, half).astype(jnp.float32) * (-2.0 * math.log(ROPE_BASE) / head)
    )
    sign = jnp.where(lane < half, -1.0, 1.0)

    targets = jnp.minimum(span, last - stretch)
    targets += (to_relay > 0).astype(jnp.int32) + (passed > 0).astype(jnp.int32)

    def wait_for_targets():
        @pl.when(targets > 0)
        def _():
            pl.semaphore_wait(barrier, targets)

        each_by_relay(lambda copy: copy.start())

    pl.when(jnp.logical_not(ahead))(wait_for_targets)

    @pl.when((uly == 1) & (to_relay == 0))
    def _():
        each_send(lambda copy: copy.start(), from_hbm)

    for copy in own_copies:
        copy.wait()

    @pl.when((uly == 0) & jnp.logical_not(ahead))
    def _():
        each_send(lambda copy: copy.start(), from_vmem)

    parts = angle_parts(stretch, rows, span, frequency)
    for copy in gain_copies:
        copy.wait()
    q_gain, k_gain = gains[0] * math.sqrt(head), gains[1] * math.sqrt(head)
    q_swap, k_swap = sign * pltpu.roll(q_gain, half, 1), sign * pltpu.roll(k_gain, half, 1)
    for d in range(span + 1):
        cosine, sine = rope_table(parts, d, rows)
        tab[d + 1, 0], tab[d + 1, 1] = cosine * k_gain, sine * k_swap
        if d == 0:
            tab[0, 0], tab[0, 1] = cosine * q_gain, sine * q_swap

    row = lax.broadcasted_iota(jnp.int32, (rows, rows), 0)
    col = lax.broadcasted_iota(jnp.int32, (rows, rows), 1)
    own = col <= row
    contract = (((1,), (1,)), ((), ()))
    from_lane = lax.broadcasted_iota(jnp.int32, (head, head), 0)
    to_lane = lax.broadcasted_iota(jnp.int32, (head, head), 1)
    swap = (from_lane == lax.rem(to_lane + half, head)).astype(jnp.float32)
    swap = swap.astype(jnp.bfloat16)

    @pl.when((uly == 1) & (to_relay > 0))
    def _():
        each_send(lambda copy: copy.start(), from_hbm)

    for h in range(kv_heads):
        k_own[h] = rotate(
            kv_own[0, :, h * head : (h + 1) * head], tab[1, 0], tab[1, 1], swap
        )
        values = v_last if h == kv_heads - 1 else v_cat.at[h]
        values[:rows, :head] = kv_own[1, :, h * head : (h + 1) * head]
        values[:, head:] = jnp.ones((values.shape[0], head), jnp.bfloat16)
    for h in range(kv_heads):
        if h == 0:

            @pl.when(ahead)
            def _():
                wait_for_targets()
                each_send(lambda copy: copy.start(), from_vmem)

        if h == kv_heads - 1:
            for late in range(kv_heads):
                pass_on(late, stretch == 2)
        q_copies[h].wait()
        keys = k_own[h]
        for g in range(group):
            at = slice(g * rows, (g + 1) * rows)
            q_rot[h, at] = rotate(
                q_buf[h, :, g * head : (g + 1) * head], tab[0, 0], tab[0, 1], swap
            )
            scores = lax.dot_general(
                q_rot[h, at], keys, contract, preferred_element_type=jnp.float32
            )
            tiles[h, 0, at] = jnp.where(own, scores, NEG_FILL)

    scale = math.log2(math.e) / math.sqrt(head)
    keep = col <= row + jnp.where(stretch >= span, 0, rows)
    bias = [
        jnp.where(stretch >= d, 0.0, NEG_FILL).astype(jnp.float32)
        for d in range(1, span)
    ]

    def arrived(h, i):
        for d in range(1, span + 1):
            remote(d, h, i, from_hbm[i]).wait_recv()

    def turn(h):
        for d in range(1, span + 1):
            k_far[h, (d - 1) * rows : d * rows] = rotate(
                kv_prev[d - 1, 0, h], tab[d + 1, 0], tab[d + 1, 1], swap
            )

    def score(h):
        for first in range(0, group, 4):
            at = slice(first * rows, (first + 4) * rows)
            scores = lax.dot_general(
                q_rot[h, at], k_far[h], contract, preferred_element_type=jnp.float32
            )
            tiles[h, 0, at] = jnp.where(
                jnp.concatenate([keep] * 4), tiles[h, 0, at], scores[:, (span - 1) * rows :]
            )
            for d in range(1, span):
                tiles[h, d, at] = scores[:, (d - 1) * rows : d * rows] + bias[d - 1]

    def weigh(h):
        for g in range(group):
            at = slice(g * rows, (g + 1) * rows)
            parts = [tiles[h, d, at] for d in range(span)]
            top = jnp.max(functools.reduce(jnp.maximum, parts), axis=-1, keepdims=True)
            for d in range(span):
                out = w_last if h == kv_heads - 1 else weights.at[h]
                out[d, at] = jnp.exp2((parts[d] - top) * scale).astype(jnp.bfloat16)

    def join(h):
        values = v_last if h == kv_heads - 1 else v_cat.at[h]
        for d in range(1, span + 1):
            values[d * rows : (d + 1) * rows, :head] = kv_prev[d - 1, 1, h]

    def mix(h):
        if h < kv_heads - 1:
            join(h)
            mix_head(weights.at[h], v_cat.at[h], o_ref, h * width, group, None)

    stages = [(0, lambda h: arrived(h, 0)), (0, turn), (1, score), (2, weigh)]
    stages += [(kv_heads, lambda h: arrived(h, 1)), (kv_heads, mix)]
    for step in range(-1, 2 * kv_heads):
        for lag, stage in stages:
            if 0 <= step - lag < kv_heads:
                stage(step - lag)
        for h in range(kv_heads):
            if step == -1:
                pass_on(h, stretch != 2)
    join(kv_heads - 1)

    each_by_relay(lambda copy: copy.wait_send())
    for h in range(kv_heads):

        @pl.when(h >= kv_heads - passed)
        def _(h=h):
            to_target(h).wait_send()

    @pl.when(uly == 1)
    def _():
        each_send(lambda copy: copy.wait_send(), from_hbm)

    @pl.when(uly == 0)
    def _():
        each_send(lambda copy: copy.wait_send(), from_vmem)


def in_hbm(array):
    return pltpu.with_memory_space_constraint(array, pltpu.HBM)


def local(query_proj, key_proj, value_projection, query_gain, key_gain):
    cycle = lax.axis_size("blk")
    span = max(1, cycle // 64)
    rows, head = query_proj.shape[0], query_gain.shape[0]
    kv_heads = key_proj.shape[1] // head
    group = query_proj.shape[1] // head // kv_heads
    bf16, f32 = jnp.bfloat16, jnp.float32
    vmem = pl.BlockSpec(memory_space=pltpu.VMEM)
    hbm = pl.BlockSpec(memory_space=pltpu.HBM)
    most = (kv_heads - 1) * group * head
    o_most, w_last, v_last = pl.pallas_call(
        functools.partial(kernel, cycle, span, kv_heads, group),
        out_shape=[
            jax.ShapeDtypeStruct((rows, most), bf16),
            jax.ShapeDtypeStruct((span, group * rows, rows), bf16),
            jax.ShapeDtypeStruct(((span + 1) * rows, 2 * head), bf16),
        ],
        in_specs=[hbm] * 5,
        out_specs=[vmem] * 3,
        scratch_shapes=[
            pltpu.VMEM((kv_heads, rows, group * head), bf16),
            pltpu.VMEM((2, rows, kv_heads * head), bf16),
            pltpu.VMEM((span, 2, kv_heads, rows, head), bf16),
            pltpu.VMEM((kv_heads, group * rows, head), bf16),
            pltpu.VMEM((kv_heads, rows, head), bf16),
            pltpu.VMEM((kv_heads, span * rows, head), bf16),
            pltpu.VMEM((kv_heads, (span + 1) * rows, 2 * head), bf16),
            pltpu.VMEM((kv_heads, span, group * rows, rows), f32),
            pltpu.VMEM((kv_heads, span, group * rows, rows), bf16),
            pltpu.VMEM((span + 2, 2, rows, head), f32),
            pltpu.VMEM((2, 1, head), f32),
            pltpu.VMEM((kv_heads, rows, head), bf16),
            pltpu.SemaphoreType.DMA((kv_heads,)),
            pltpu.SemaphoreType.DMA((2,)),
            pltpu.SemaphoreType.DMA((2,)),
            pltpu.SemaphoreType.DMA((span, 2, kv_heads)),
            pltpu.SemaphoreType.DMA((span, 2, kv_heads)),
            pltpu.SemaphoreType.DMA((kv_heads,)),
            pltpu.SemaphoreType.DMA((kv_heads,)),
        ],
        compiler_params=pltpu.CompilerParams(
            collective_id=0, has_side_effects=True, vmem_limit_bytes=24 * 1024 * 1024
        ),
        name="window_attention",
    )(
        in_hbm(query_proj),
        in_hbm(key_proj),
        in_hbm(value_projection),
        in_hbm(query_gain.reshape(1, head)),
        in_hbm(key_gain.reshape(1, head)),
    )
    return pl.pallas_call(
        functools.partial(finish, group),
        out_shape=jax.ShapeDtypeStruct(query_proj.shape, bf16),
        in_specs=[vmem] * 3,
        out_specs=hbm,
        scratch_shapes=[
            pltpu.VMEM((rows, group * head), bf16),
            pltpu.SemaphoreType.DMA((5,)),
        ],
        compiler_params=pltpu.CompilerParams(vmem_limit_bytes=8 * 1024 * 1024),
        name="last_heads",
    )(o_most, w_last, v_last)


def solution(mesh):
    rows = P(("groups", "blk", "uly"), None)
    return jax.shard_map(
        local,
        mesh=mesh,
        in_specs=(rows, rows, rows, P(), P()),
        out_specs=rows,
        check_vma=False,
    )
```

```python
import functools
import math

import jax
import jax.numpy as jnp
from jax import lax
from jax.experimental import pallas as pl
from jax.experimental.pallas import tpu as pltpu
from jax.sharding import PartitionSpec as P

NEG_FILL = -1e30
ROPE_BASE = 1000000.0
EPS = 1e-06
MESH = pl.DeviceIdType.MESH


def angle_parts(stretch, rows, span, frequency):
    steps = rows // 8
    count = 8 + steps + 8 * pl.cdiv(span + 1, 8)
    index = lax.broadcasted_iota(jnp.int32, (count, frequency.shape[1]), 0)
    offset = jnp.where(
        index < 8,
        index,
        jnp.where(index < 8 + steps, (index - 8) * 8, (stretch - (index - 8 - steps)) * rows),
    )
    angle = offset.astype(jnp.float32) * frequency
    return jnp.cos(angle), jnp.sin(angle)


def rope_table(parts, d, rows):
    cosine, sine = parts
    steps = rows // 8
    fine_cos, fine_sin = cosine[:8], sine[:8]
    eights_cos, eights_sin = cosine[8 : 8 + steps], sine[8 : 8 + steps]
    at = 8 + steps + d
    first_cos, first_sin = cosine[at : at + 1], sine[at : at + 1]
    coarse_cos = eights_cos * first_cos - eights_sin * first_sin
    coarse_sin = eights_sin * first_cos + eights_cos * first_sin
    cosines, sines = [], []
    for j in range(steps):
        cos_j, sin_j = coarse_cos[j : j + 1], coarse_sin[j : j + 1]
        cosines.append(cos_j * fine_cos - sin_j * fine_sin)
        sines.append(sin_j * fine_cos + cos_j * fine_sin)
    return jnp.concatenate(cosines), jnp.concatenate(sines)


def rotate(x, table_a, table_b, swap):
    swapped = jnp.dot(x, swap, preferred_element_type=jnp.float32)
    x = x.astype(jnp.float32)
    r = lax.rsqrt(jnp.sum(x * x, axis=-1, keepdims=True) + x.shape[1] * EPS)
    return ((x * table_a + swapped * table_b) * r).astype(jnp.bfloat16)


def mix_head(weights, v_cat, o_ref, column, group, ready):
    span, rows, head = weights.shape[0], weights.shape[2], v_cat.shape[1] // 2
    row = lax.broadcasted_iota(jnp.int32, (rows, rows), 0)
    col = lax.broadcasted_iota(jnp.int32, (rows, rows), 1)
    own_mask = (col <= row).astype(jnp.float32).astype(jnp.bfloat16)
    far_mask = 1.0 - own_mask
    values = v_cat[...]
    heads = max(1, group // (2 if ready is None else 4))
    for part in range(group // heads):
        block = slice(part * heads * rows, (part + 1) * heads * rows)
        merged = weights[0, block]
        spread = [merged * jnp.concatenate([own_mask] * heads)]
        spread += [weights[d, block] for d in range(1, span)]
        spread += [merged * jnp.concatenate([far_mask] * heads)]
        mixed = jnp.dot(
            jnp.concatenate(spread, axis=1), values, preferred_element_type=jnp.float32
        )
        for g in range(heads):
            piece = mixed[g * rows : (g + 1) * rows]
            at = column + (part * heads + g) * head
            o_ref[:, at : at + head] = (piece[:, :head] / piece[:, head:]).astype(
                o_ref.dtype
            )
        if ready is not None:
            ready(part)


def finish(group, o_most, w_last, v_last, o_hbm, o_last, sem):
    width, most = o_last.shape[1], o_most.shape[1]
    copies = [pltpu.make_async_copy(o_most, o_hbm.at[:, pl.ds(0, most)], sem.at[0])]
    copies[0].start()
    quarter = width // 4

    def ready(part):
        copy = pltpu.make_async_copy(
            o_last.at[:, pl.ds(part * quarter, quarter)],
            o_hbm.at[:, pl.ds(most + part * quarter, quarter)],
            sem.at[1 + part],
        )
        copy.start()
        copies.append(copy)

    mix_head(w_last, v_last, o_last, 0, group, ready)
    for copy in copies:
        copy.wait()


def kernel(
    cycle, span, kv_heads, group,
    q_hbm, k_hbm, v_hbm, qg_hbm, kg_hbm, o_ref, w_last, v_last,
    q_buf, kv_own, kv_prev, q_rot, k_own, k_far, v_cat, tiles, weights, tab, gains,
    relay_buf, q_sem, own_sem, gain_sem, send_sem, recv_sem, pass_sem, relay_sem,
):
    rows, head = k_hbm.shape[0], qg_hbm.shape[1]
    width = group * head
    blk, uly = lax.axis_index("blk"), lax.axis_index("uly")
    last = 2 * cycle - 1
    stretch = jnp.where(uly == 0, blk, last - blk)
    first_group = lax.axis_index("groups") == 0
    ahead = first_group & (stretch == 0)

    def device_of(index):
        low = index < cycle
        return {"blk": jnp.where(low, index, last - index), "uly": jnp.where(low, 0, 1)}

    barrier = pltpu.get_barrier_semaphore()

    def greet(index):
        pl.semaphore_signal(
            barrier, inc=1, device_id=device_of(index), device_id_type=MESH
        )

    for d in range(1, span + 1):
        pl.when(stretch >= d)(functools.partial(greet, stretch - d))

    def count_between(relay):
        high = (relay >= cycle) & (relay + 2 <= last) & (lax.rem(relay, 2) == 0)
        return jnp.where(high, kv_heads - 1, jnp.where(first_group & (relay == 2), kv_heads - 1, 0))

    relay = jnp.where(stretch == 0, 2, jnp.maximum(stretch - 1, 0))
    odd = (lax.rem(stretch, 2) == 1) & (stretch > cycle)
    to_relay = jnp.where(odd | (stretch == 0), count_between(relay), 0)
    passed = count_between(stretch)
    source = jnp.where(stretch == 2, 0, jnp.minimum(stretch + 1, last))
    target = jnp.where(stretch == 2, 1, jnp.minimum(stretch + 2, last))
    passer = jnp.where(stretch == 1, 2, jnp.maximum(stretch - 2, 0))
    fed = (stretch == 1) | ((lax.rem(stretch, 2) == 0) & (stretch > cycle + 1))
    from_relay = jnp.where(fed, count_between(passer), 0)

    pl.when(from_relay > 0)(functools.partial(greet, passer))
    pl.when(passed > 0)(functools.partial(greet, source))

    own_copies = [
        pltpu.make_async_copy(src, kv_own.at[i], own_sem.at[i])
        for i, src in enumerate((k_hbm, v_hbm))
    ]
    q_copies = [
        pltpu.make_async_copy(
            q_hbm.at[:, pl.ds(h * width, width)], q_buf.at[h], q_sem.at[h]
        )
        for h in range(kv_heads)
    ]
    gain_copies = [
        pltpu.make_async_copy(src, gains.at[i], gain_sem.at[i])
        for i, src in enumerate((qg_hbm, kg_hbm))
    ]

    def remote(d, h, i, src):
        return pltpu.make_async_remote_copy(
            src_ref=src.at[:, pl.ds(h * head, head)],
            dst_ref=kv_prev.at[d - 1, i, h],
            send_sem=send_sem.at[d - 1, i, h],
            recv_sem=recv_sem.at[d - 1, i, h],
            device_id=device_of(stretch + d),
            device_id_type=MESH,
        )

    from_hbm = (k_hbm, v_hbm)
    from_vmem = (kv_own.at[0], kv_own.at[1])

    def each_send(act, sources):
        for i in range(2):
            for h in range(kv_heads):
                for d in range(1, span + 1):
                    sent = stretch + d <= last
                    if d == 1 and i == 1:
                        sent = sent & (h < kv_heads - to_relay)

                    @pl.when(sent)
                    def _(d=d, h=h, i=i):
                        act(remote(d, h, i, sources[i]))

    def to_target(h):
        return pltpu.make_async_remote_copy(
            src_ref=relay_buf.at[h],
            dst_ref=kv_prev.at[0, 1, h],
            send_sem=pass_sem.at[h],
            recv_sem=recv_sem.at[0, 1, h],
            device_id=device_of(target),
            device_id_type=MESH,
        )

    def by_relay(h):
        return pltpu.make_async_remote_copy(
            src_ref=v_hbm.at[:, pl.ds(h * head, head)],
            dst_ref=relay_buf.at[h],
            send_sem=send_sem.at[0, 1, h],
            recv_sem=relay_sem.at[h],
            device_id=device_of(relay),
            device_id_type=MESH,
        )

    def each_by_relay(act):
        for h in range(kv_heads):

            @pl.when(h >= kv_heads - to_relay)
            def _(h=h):
                act(by_relay(h))

    def pass_on(h, when):
        @pl.when(when & (h >= kv_heads - passed))
        def _():
            by_relay(h).wait_recv()
            to_target(h).start()

    for copy in own_copies:
        copy.start()

    @pl.when(uly == 0)
    def _():
        for copy in gain_copies + q_copies:
            copy.start()

    for d in range(1, span + 1):

        @pl.when(stretch < d)
        def _(d=d):
            for i in range(2):
                for h in range(kv_heads):
                    pltpu.make_async_copy(
                        from_hbm[i].at[:, pl.ds(h * head, head)],
                        kv_prev.at[d - 1, i, h],
                        recv_sem.at[d - 1, i, h],
                    ).start()

    half = head // 2
    lane = lax.broadcasted_iota(jnp.int32, (1, head), 1)
    frequency = jnp.exp(
        lax.rem(lane, half).astype(jnp.float32) * (-2.0 * math.log(ROPE_BASE) / head)
    )
    sign = jnp.where(lane < half, -1.0, 1.0)

    targets = jnp.minimum(span, last - stretch)
    targets += (to_relay > 0).astype(jnp.int32) + (passed > 0).astype(jnp.int32)

    def wait_for_targets():
        @pl.when(targets > 0)
        def _():
            pl.semaphore_wait(barrier, targets)

        each_by_relay(lambda copy: copy.start())

    pl.when(jnp.logical_not(ahead))(wait_for_targets)

    @pl.when((uly == 1) & (to_relay == 0))
    def _():
        each_send(lambda copy: copy.start(), from_hbm)

    @pl.when(uly == 1)
    def _():
        for copy in gain_copies + q_copies:
            copy.start()

    for copy in own_copies:
        copy.wait()

    @pl.when((uly == 0) & jnp.logical_not(ahead))
    def _():
        each_send(lambda copy: copy.start(), from_vmem)

    parts = angle_parts(stretch, rows, span, frequency)
    for copy in gain_copies:
        copy.wait()
    q_gain, k_gain = gains[0] * math.sqrt(head), gains[1] * math.sqrt(head)
    q_swap, k_swap = sign * pltpu.roll(q_gain, half, 1), sign * pltpu.roll(k_gain, half, 1)
    for d in range(span + 1):
        cosine, sine = rope_table(parts, d, rows)
        tab[d + 1, 0], tab[d + 1, 1] = cosine * k_gain, sine * k_swap
        if d == 0:
            tab[0, 0], tab[0, 1] = cosine * q_gain, sine * q_swap

    row = lax.broadcasted_iota(jnp.int32, (rows, rows), 0)
    col = lax.broadcasted_iota(jnp.int32, (rows, rows), 1)
    own = col <= row
    contract = (((1,), (1,)), ((), ()))
    from_lane = lax.broadcasted_iota(jnp.int32, (head, head), 0)
    to_lane = lax.broadcasted_iota(jnp.int32, (head, head), 1)
    swap = (from_lane == lax.rem(to_lane + half, head)).astype(jnp.float32)
    swap = swap.astype(jnp.bfloat16)

    for h in range(kv_heads):
        k_own[h] = rotate(
            kv_own[0, :, h * head : (h + 1) * head], tab[1, 0], tab[1, 1], swap
        )
        values = v_last if h == kv_heads - 1 else v_cat.at[h]
        values[:rows, :head] = kv_own[1, :, h * head : (h + 1) * head]
        values[:, head:] = jnp.ones((values.shape[0], head), jnp.bfloat16)
    for h in range(kv_heads):
        if h == 0:

            @pl.when(ahead)
            def _():
                wait_for_targets()
                each_send(lambda copy: copy.start(), from_vmem)

        if h == kv_heads - 1:
            for late in range(kv_heads):
                pass_on(late, stretch == 2)
        q_copies[h].wait()
        keys = k_own[h]
        for g in range(group):
            if h == 0 and g == 0:

                @pl.when((uly == 1) & (to_relay > 0))
                def _():
                    each_send(lambda copy: copy.start(), from_hbm)

            at = slice(g * rows, (g + 1) * rows)
            q_rot[h, at] = rotate(
                q_buf[h, :, g * head : (g + 1) * head], tab[0, 0], tab[0, 1], swap
            )
            scores = lax.dot_general(
                q_rot[h, at], keys, contract, preferred_element_type=jnp.float32
            )
            tiles[h, 0, at] = jnp.where(own, scores, NEG_FILL)

    scale = math.log2(math.e) / math.sqrt(head)
    keep = col <= row + jnp.where(stretch >= span, 0, rows)
    bias = [
        jnp.where(stretch >= d, 0.0, NEG_FILL).astype(jnp.float32)
        for d in range(1, span)
    ]

    def arrived(h, i):
        for d in range(1, span + 1):
            remote(d, h, i, from_hbm[i]).wait_recv()

    def turn(h):
        for d in range(1, span + 1):
            k_far[h, (d - 1) * rows : d * rows] = rotate(
                kv_prev[d - 1, 0, h], tab[d + 1, 0], tab[d + 1, 1], swap
            )

    def score(h):
        for first in range(0, group, 4):
            at = slice(first * rows, (first + 4) * rows)
            scores = lax.dot_general(
                q_rot[h, at], k_far[h], contract, preferred_element_type=jnp.float32
            )
            tiles[h, 0, at] = jnp.where(
                jnp.concatenate([keep] * 4), tiles[h, 0, at], scores[:, (span - 1) * rows :]
            )
            for d in range(1, span):
                tiles[h, d, at] = scores[:, (d - 1) * rows : d * rows] + bias[d - 1]

    def weigh(h):
        for g in range(group):
            at = slice(g * rows, (g + 1) * rows)
            parts = [tiles[h, d, at] for d in range(span)]
            top = jnp.max(functools.reduce(jnp.maximum, parts), axis=-1, keepdims=True)
            for d in range(span):
                out = w_last if h == kv_heads - 1 else weights.at[h]
                out[d, at] = jnp.exp2((parts[d] - top) * scale).astype(jnp.bfloat16)

    def join(h):
        values = v_last if h == kv_heads - 1 else v_cat.at[h]
        for d in range(1, span + 1):
            values[d * rows : (d + 1) * rows, :head] = kv_prev[d - 1, 1, h]

    def mix(h):
        if h < kv_heads - 1:
            join(h)
            mix_head(weights.at[h], v_cat.at[h], o_ref, h * width, group, None)

    stages = [(0, lambda h: arrived(h, 0)), (0, turn), (1, score), (2, weigh)]
    stages += [(kv_heads, lambda h: arrived(h, 1)), (kv_heads, mix)]
    for step in range(-1, 2 * kv_heads):
        for lag, stage in stages:
            if 0 <= step - lag < kv_heads:
                stage(step - lag)
        for h in range(kv_heads):
            if step == -1:
                pass_on(h, stretch != 2)
    join(kv_heads - 1)

    each_by_relay(lambda copy: copy.wait_send())
    for h in range(kv_heads):

        @pl.when(h >= kv_heads - passed)
        def _(h=h):
            to_target(h).wait_send()

    @pl.when(uly == 1)
    def _():
        each_send(lambda copy: copy.wait_send(), from_hbm)

    @pl.when(uly == 0)
    def _():
        each_send(lambda copy: copy.wait_send(), from_vmem)


def in_hbm(array):
    return pltpu.with_memory_space_constraint(array, pltpu.HBM)


def local(query_proj, key_proj, value_projection, query_gain, key_gain):
    cycle = lax.axis_size("blk")
    span = max(1, cycle // 64)
    rows, head = query_proj.shape[0], query_gain.shape[0]
    kv_heads = key_proj.shape[1] // head
    group = query_proj.shape[1] // head // kv_heads
    bf16, f32 = jnp.bfloat16, jnp.float32
    vmem = pl.BlockSpec(memory_space=pltpu.VMEM)
    hbm = pl.BlockSpec(memory_space=pltpu.HBM)
    most = (kv_heads - 1) * group * head
    o_most, w_last, v_last = pl.pallas_call(
        functools.partial(kernel, cycle, span, kv_heads, group),
        out_shape=[
            jax.ShapeDtypeStruct((rows, most), bf16),
            jax.ShapeDtypeStruct((span, group * rows, rows), bf16),
            jax.ShapeDtypeStruct(((span + 1) * rows, 2 * head), bf16),
        ],
        in_specs=[hbm] * 5,
        out_specs=[vmem] * 3,
        scratch_shapes=[
            pltpu.VMEM((kv_heads, rows, group * head), bf16),
            pltpu.VMEM((2, rows, kv_heads * head), bf16),
            pltpu.VMEM((span, 2, kv_heads, rows, head), bf16),
            pltpu.VMEM((kv_heads, group * rows, head), bf16),
            pltpu.VMEM((kv_heads, rows, head), bf16),
            pltpu.VMEM((kv_heads, span * rows, head), bf16),
            pltpu.VMEM((kv_heads, (span + 1) * rows, 2 * head), bf16),
            pltpu.VMEM((kv_heads, span, group * rows, rows), f32),
            pltpu.VMEM((kv_heads, span, group * rows, rows), bf16),
            pltpu.VMEM((span + 2, 2, rows, head), f32),
            pltpu.VMEM((2, 1, head), f32),
            pltpu.VMEM((kv_heads, rows, head), bf16),
            pltpu.SemaphoreType.DMA((kv_heads,)),
            pltpu.SemaphoreType.DMA((2,)),
            pltpu.SemaphoreType.DMA((2,)),
            pltpu.SemaphoreType.DMA((span, 2, kv_heads)),
            pltpu.SemaphoreType.DMA((span, 2, kv_heads)),
            pltpu.SemaphoreType.DMA((kv_heads,)),
            pltpu.SemaphoreType.DMA((kv_heads,)),
        ],
        compiler_params=pltpu.CompilerParams(
            collective_id=0, has_side_effects=True, vmem_limit_bytes=24 * 1024 * 1024
        ),
        name="window_attention",
    )(
        in_hbm(query_proj),
        in_hbm(key_proj),
        in_hbm(value_projection),
        in_hbm(query_gain.reshape(1, head)),
        in_hbm(key_gain.reshape(1, head)),
    )
    return pl.pallas_call(
        functools.partial(finish, group),
        out_shape=jax.ShapeDtypeStruct(query_proj.shape, bf16),
        in_specs=[vmem] * 3,
        out_specs=hbm,
        scratch_shapes=[
            pltpu.VMEM((rows, group * head), bf16),
            pltpu.SemaphoreType.DMA((5,)),
        ],
        compiler_params=pltpu.CompilerParams(vmem_limit_bytes=8 * 1024 * 1024),
        name="last_heads",
    )(o_most, w_last, v_last)


def solution(mesh):
    rows = P(("groups", "blk", "uly"), None)
    return jax.shard_map(
        local,
        mesh=mesh,
        in_specs=(rows, rows, rows, P(), P()),
        out_specs=rows,
        check_vma=False,
    )
```
